128 devices in a mesh: chan: 8 (over y, core), inp: 16 (over z, x).
Axes of the slice: x: 4, y: 4, z: 4, core: 2. Of those that a mesh axis runs over, the one named last changes fastest.
Arguments:
- voltages: bfloat16 [1024, 262144], P('inp', 'chan'), may hold values from -64 to 64
- tile_table: int32 [144, 2], replicated, may hold values from -1 to 15, as said below
Outputs:
- coherence: float32 [512, 144, 64, 128], P('chan', 'inp')
The draws below stay inside these ranges and needn't reach their ends.
Inputs may be any that keep to these rules, and one draw needn't show every extreme that they name: `tile_table`: rows 9 d to 9 d + 8 are the slots whose tiles the device at index d along inp outputs. Every pair (a, b) with 0 <= a <= b < 16 stands in exactly one row, and every other row is (-1, -1); the pairs are spread over the rows in any order.
All inputs are finite; a program needn't handle non-finite values.
Results may differ from the reference program's by a relative error of at most 0.0058.
Values may be sent and summed in bfloat16 or wider, within the bound.
No kernel may reach another device: no remote copies, remote signals or barrier semaphores. Data moves between devices by JAX's collectives and lax.ppermute only.
A program may use at most 128 MiB of HBM per device.

```python
import math
import jax
import jax.numpy as jnp
import numpy as np
from jax import lax

NI = 1024
L = 2048
NCH = 512
TAPS = 4
NB = 64
FRAMES = 128
NSAMP = 262144
N_INP = 16


def draw_voltages(key, part):
    key_noise = jax.random.fold_in(key, 0)
    thermal = jax.random.normal(key_noise, (NI, NSAMP), jnp.float32)
    values = thermal
    return jnp.clip(values, -64.0, 64.0).astype(jnp.bfloat16)


def draw_tile_table(key, part):
    tile_count = N_INP * (N_INP + 1) // 2
    slot_count = N_INP * (N_INP // 2 + 1)
    upper_rows, upper_cols = np.triu_indices(N_INP)
    pair_list = np.concatenate([np.stack([upper_rows, upper_cols], axis=1), -np.ones((slot_count - tile_count, 2), np.int64)], axis=0)
    pair_list = jnp.asarray(pair_list.astype(np.int32))
    shuffle = jax.random.permutation(key, slot_count)
    return pair_list[shuffle]


def setup_inputs(seed: int = 0) -> dict:
    keys = jax.random.split(jax.random.key(seed), 3)
    return {
        "voltages": draw_voltages(jax.random.fold_in(keys[2], 71), 0),
        "tile_table": draw_tile_table(jax.random.fold_in(keys[2], 71), 0),
    }


def filter_window():
    positions = jnp.arange(TAPS * L, dtype=jnp.float32)
    shape_sinc = jnp.sinc((positions - TAPS * L / 2.0) / L)
    tapering = 0.5 - 0.5 * jnp.cos(2.0 * math.pi * positions / (TAPS * L))
    return (shape_sinc * tapering).reshape(TAPS, L)

def transform_table():
    samples = jnp.arange(L, dtype=jnp.int32)[:, None]
    channels = jnp.arange(NCH, dtype=jnp.int32)[None, :]
    phases = samples * channels % L
    angles = phases.astype(jnp.float32) * (2.0 * math.pi / L)
    return jnp.stack([jnp.cos(angles), -jnp.sin(angles)], axis=2).reshape(L, 2 * NCH).astype(jnp.bfloat16)

def rotate_parts(rows):
    half_width = rows.shape[-1] // 2
    return jnp.concatenate([-rows[..., half_width:], rows[..., :half_width]], axis=-1)

def channel_tiles(columns, channel_power, first_all, second_all, present_all, block_width, frame_total):
    partner = jnp.concatenate([columns, rotate_parts(columns)], axis=0)
    gram_full = lax.dot_general(columns, partner, (((1,), (1,)), ((), ())), preferred_element_type=jnp.float32)
    block_count = columns.shape[0] // block_width
    gram_grid = gram_full.reshape(block_count, block_width, 2, block_count, block_width)
    picked = gram_grid[first_all, :, :, second_all, :]
    picked = picked.reshape(first_all.shape[0], block_width, 2 * block_width)
    power_grid = channel_power.reshape(block_count, block_width)
    inverse = present_all[:, None, None] / (frame_total * jnp.sqrt(power_grid[first_all][:, :, None] * power_grid[second_all][:, None, :]))
    return picked * jnp.concatenate([inverse, inverse], axis=2)

def reference(voltages, tile_table):
    blocks = voltages.reshape(NI, FRAMES, L)
    extended = jnp.concatenate([blocks, jnp.zeros((NI, TAPS - 1, L), voltages.dtype)], axis=1)
    window = filter_window()
    filtered = jnp.zeros((NI, FRAMES, L), jnp.float32)
    for tap_index in range(TAPS):
        filtered = filtered + extended[:, tap_index:tap_index + FRAMES, :].astype(jnp.float32) * window[tap_index]
    filtered = filtered.astype(jnp.bfloat16).reshape(NI * FRAMES, L)
    spectra = jnp.dot(filtered, transform_table(), preferred_element_type=jnp.float32).astype(jnp.bfloat16)
    arranged = spectra.reshape(NI, FRAMES, NCH, 2).transpose(2, 0, 3, 1).reshape(NCH, NI, 2 * FRAMES)
    autopower = lax.optimization_barrier(jnp.sum(jnp.square(arranged.astype(jnp.float32)), axis=2)) / FRAMES + 1e-06
    first_all = jnp.maximum(tile_table[:, 0], 0).astype(jnp.int32)
    second_all = jnp.maximum(tile_table[:, 1], 0).astype(jnp.int32)
    present_all = (tile_table[:, 0] >= 0).astype(jnp.float32)

    def per_channel(pair_in):
        return channel_tiles(pair_in[0], pair_in[1], first_all, second_all, present_all, NB, FRAMES)
    return lax.map(per_channel, (arranged, autopower))
```

```python
import math

import jax
import jax.numpy as jnp
import numpy as np
from jax import lax
from jax.experimental import pallas as pl
from jax.experimental.pallas import tpu as pltpu
from jax.sharding import PartitionSpec as P

L = 2048
NCH = 512
TAPS = 4
LANES = 128
STEP = 4
COARSE = 16
EVERY = ("chan", "inp")


def filter_window():
    positions = np.arange(TAPS * L, dtype=np.float64)
    tapering = 0.5 - 0.5 * np.cos(2.0 * math.pi * positions / (TAPS * L))
    shape_sinc = np.sinc((positions - TAPS * L / 2.0) / L)
    return (shape_sinc * tapering).reshape(TAPS, L).astype(np.float32)


def twiddle_factors():
    samples = np.arange(L)[None, :]
    coarse = (COARSE * np.arange(NCH // COARSE)[:, None] * samples) % L
    rows = np.arange(2 * COARSE)[:, None]
    fine = ((rows // 2) * samples + (rows % 2) * (L // 4)) % L
    unit = 2.0 * math.pi / L
    tables = [np.cos(coarse * unit), np.sin(coarse * unit), np.cos(fine * unit), np.sin(fine * unit)]
    return [t.astype(np.float32) for t in tables]


def build_table(coarse_cos, coarse_sin, fine_cos, fine_sin, table):
    rows = 2 * COARSE

    def column(j, carry):
        lanes = pl.ds(pl.multiple_of(j * LANES, LANES), LANES)
        fc = fine_cos[:, lanes]
        fs = fine_sin[:, lanes]
        for a in range(NCH // COARSE):
            part = coarse_cos[a : a + 1, lanes] * fc - coarse_sin[a : a + 1, lanes] * fs
            table[a * rows : (a + 1) * rows, lanes] = part.astype(jnp.bfloat16)
        return carry

    lax.fori_loop(0, L // LANES, column, 0)


def filter_frames(window, current, following, filtered):
    width = current.shape[0]

    def column(j, carry):
        taps = [window[k : k + 1, pl.ds(pl.multiple_of(j * LANES, LANES), LANES)] for k in range(TAPS)]
        for r in range(0, width, 16):
            rows = slice(r, r + 16)
            frames = []
            for f in range(STEP + TAPS - 1):
                source, at = (current, f) if f < STEP else (following, f - STEP)
                lanes = pl.ds(pl.multiple_of(j * LANES + at * L, LANES), LANES)
                frames.append(source[rows, lanes].astype(jnp.float32))
            for f in range(STEP):
                total = frames[f] * taps[0]
                for k in range(1, TAPS):
                    total = total + frames[f + k] * taps[k]
                filtered[f * width + r : f * width + r + 16, pl.ds(pl.multiple_of(j * LANES, LANES), LANES)] = (
                    total.astype(jnp.bfloat16)
                )
        return carry

    lax.fori_loop(0, L // LANES, column, 0)


def transform(table, filtered, spectra):
    rows = 256

    def chunk(i, carry):
        at = pl.ds(pl.multiple_of(i * rows, rows), rows)
        product = lax.dot_general(
            table[at, :], filtered[...], (((1,), (1,)), ((), ())), preferred_element_type=jnp.float32
        )
        spectra[at, :] = product.astype(jnp.bfloat16)
        return carry

    lax.fori_loop(0, 2 * NCH // rows, chunk, 0)


def early_kernel(cc, cs, fc, fs, window, current, following, spectra, table, filtered):
    @pl.when(pl.program_id(0) == 0)
    def _():
        build_table(cc, cs, fc, fs, table)

    filter_frames(window, current, following, filtered)
    transform(table, filtered, spectra)


def late_kernel(table, window, current, following, earlier, spectra, filtered):
    del earlier
    filter_frames(window, current, following, filtered)
    transform(table, filtered, spectra)


def channelize(voltages):
    width, local_len = voltages.shape
    steps = local_len // (STEP * L)
    span = STEP * L
    halo = (TAPS - 1) * L
    devices = lax.axis_size("chan")
    following = lax.ppermute(voltages[:, :halo], "chan", [(i, i - 1) for i in range(1, devices)])
    window = jnp.asarray(filter_window())
    factors = [jnp.asarray(t) for t in twiddle_factors()]
    columns = STEP * width
    whole = lambda shape: pl.BlockSpec(shape, lambda *_: (0, 0))
    spectra_shape = jax.ShapeDtypeStruct((2 * NCH, steps * columns), jnp.bfloat16)
    early, table = pl.pallas_call(
        early_kernel,
        name="channelize_early",
        grid=(steps - 1,),
        in_specs=[whole(t.shape) for t in factors]
        + [
            whole((TAPS, L)),
            pl.BlockSpec((width, span), lambda j: (0, j)),
            pl.BlockSpec((width, span), lambda j: (0, j + 1)),
        ],
        out_specs=[pl.BlockSpec((2 * NCH, columns), lambda j: (0, j)), whole((2 * NCH, L))],
        out_shape=[spectra_shape, jax.ShapeDtypeStruct((2 * NCH, L), jnp.bfloat16)],
        scratch_shapes=[pltpu.VMEM((columns, L), jnp.bfloat16)],
        cost_estimate=pl.CostEstimate(flops=3 * 10**9, bytes_accessed=12 * 2**20, transcendentals=0),
    )(*factors, window, voltages, voltages)
    return pl.pallas_call(
        late_kernel,
        name="channelize_late",
        grid=(1,),
        in_specs=[
            whole((2 * NCH, L)),
            whole((TAPS, L)),
            pl.BlockSpec((width, span), lambda j: (0, steps - 1)),
            whole((width, halo)),
            pl.BlockSpec(memory_space=pl.ANY),
        ],
        out_specs=pl.BlockSpec((2 * NCH, columns), lambda j: (0, steps - 1)),
        out_shape=spectra_shape,
        scratch_shapes=[pltpu.VMEM((columns, L), jnp.bfloat16)],
        input_output_aliases={4: 0},
        cost_estimate=pl.CostEstimate(flops=10**9, bytes_accessed=6 * 2**20, transcendentals=0),
    )(table, window, voltages, following, early)


def gram_kernel(frame_total, slots, spectra, tiles, wide, lefts, rights, row_scale, col_scale, grid_tiles):
    channel = pl.program_id(0)
    blocks = grid_tiles.shape[0]
    width = grid_tiles.shape[2]
    times = spectra.shape[0] // blocks
    pieces = spectra.shape[2] // LANES
    parts = spectra.shape[1]
    depth = times * pieces

    @pl.when(channel == 0)
    def _():
        def unpack(n, carry):
            t, b = n // blocks, n % blocks
            rows = spectra[n].astype(jnp.float32)
            for p in range(pieces):
                at = pl.multiple_of((t * pieces + p) * parts, parts)
                wide[b, pl.ds(at, parts), :] = rows[:, p * LANES : (p + 1) * LANES]
            return carry

        lax.fori_loop(0, times * blocks, unpack, 0)

    low = lax.broadcasted_iota(jnp.int32, (depth, LANES), 1) < width
    half = LANES // 2
    turn = lambda x: pltpu.roll(x, half, 1)

    def matrix(b):
        re = wide[b, pl.ds(channel * 2, depth, stride=parts), :]
        im = wide[b, pl.ds(channel * 2 + 1, depth, stride=parts), :]
        return (jnp.where(low, re, turn(im)), jnp.where(low, turn(re), im))

    def scale(power):
        return 1.0 / jnp.sqrt(power / frame_total + 1e-6)

    def build(q, carry):
        pair = [matrix(2 * q), matrix(2 * q + 1)]
        for n, halves in enumerate(pair):
            lanes = slice(n * LANES, (n + 1) * LANES)
            power = jnp.zeros((1, LANES), jnp.float32)
            for h, x in enumerate(halves):
                rolled = turn(x)
                rights[q, h * depth : (h + 1) * depth, lanes] = jnp.where(low, x, -x).astype(jnp.bfloat16)
                rights[q, (2 + h) * depth : (3 + h) * depth, lanes] = rolled.astype(jnp.bfloat16)
                power = power + jnp.sum(x * x + rolled * rolled, axis=0, keepdims=True)
            col_scale[q, :, lanes] = scale(power)
        for h in range(2):
            x, y = pair[0][h], pair[1][h]
            re = jnp.where(low, x, turn(y))
            im = jnp.where(low, turn(x), y)
            if h == 0:
                first = (re, im)
        flat = jnp.concatenate([first[0], re, first[1], im], axis=0).T
        rows = pl.ds(pl.multiple_of(q * LANES, LANES), LANES)
        lefts[rows, :] = flat.astype(jnp.bfloat16)
        row_scale[rows, :] = scale(jnp.sum(flat * flat, axis=1, keepdims=True)) / frame_total
        return carry

    lax.fori_loop(0, blocks // 2, build, 0)

    for q in range(blocks // 2):
        rows = (q + 1) * LANES
        product = jnp.dot(lefts[:rows, :], rights[q], preferred_element_type=jnp.float32)
        product = (product * row_scale[:rows, :] * col_scale[q]).astype(jnp.bfloat16)
        for a in range(2 * q + 2):
            for n in range(2):
                grid_tiles[a, 2 * q + n] = product[a * width : (a + 1) * width, n * LANES : (n + 1) * LANES]

    per_owner = tiles.shape[2]

    def pick(s, carry):
        a, b = slots[s, 0], slots[s, 1]
        tile = grid_tiles[jnp.maximum(a, 0), jnp.maximum(b, 0)]
        tiles[s // per_owner, 0, s % per_owner] = jnp.where(a >= 0, tile, jnp.zeros_like(tile))
        return carry

    lax.fori_loop(0, slots.shape[0], pick, 0, unroll=4)


def all_tiles(spectra, tile_table, blocks, width, frame_total):
    parts = spectra.shape[1]
    channels = parts // 2
    times = spectra.shape[0] // blocks
    depth = times * spectra.shape[2] // LANES
    owners = blocks
    per_owner = tile_table.shape[0] // owners

    def body(*refs):
        gram_kernel(float(frame_total), *refs)

    return pl.pallas_call(
        body,
        name="gram",
        grid_spec=pltpu.PrefetchScalarGridSpec(
            num_scalar_prefetch=1,
            grid=(channels,),
            in_specs=[pl.BlockSpec(spectra.shape, lambda c, s: (0, 0, 0))],
            out_specs=pl.BlockSpec((owners, 1, per_owner, width, 2 * width), lambda c, s: (0, c, 0, 0, 0)),
            scratch_shapes=[
                pltpu.VMEM((blocks, depth * parts, LANES), jnp.float32),
                pltpu.VMEM((blocks * width, 4 * depth), jnp.bfloat16),
                pltpu.VMEM((blocks // 2, 4 * depth, 2 * LANES), jnp.bfloat16),
                pltpu.VMEM((blocks * width, 1), jnp.float32),
                pltpu.VMEM((blocks // 2, 1, 2 * LANES), jnp.float32),
                pltpu.VMEM((blocks, blocks, width, 2 * width), jnp.bfloat16),
            ],
        ),
        out_shape=jax.ShapeDtypeStruct((owners, channels, per_owner, width, 2 * width), jnp.bfloat16),
        cost_estimate=pl.CostEstimate(flops=3 * 10**9, bytes_accessed=12 * 2**20, transcendentals=0),
    )(tile_table, spectra)


def on_device(voltages, tile_table):
    width, local_len = voltages.shape
    blocks = lax.axis_size("inp")
    devices = blocks * lax.axis_size("chan")
    frame_total = local_len // L * lax.axis_size("chan")
    spectra = channelize(voltages)
    spectra = spectra.reshape(devices, 2 * NCH // devices, spectra.shape[1])
    turned = lax.all_to_all(spectra, EVERY, 0, 0, tiled=True)
    tiles = all_tiles(turned, tile_table, blocks, width, frame_total)
    tiles = lax.all_to_all(tiles, "inp", 0, 0, tiled=True)
    return tiles.astype(jnp.float32).reshape(-1, *tiles.shape[2:])


def solution(mesh):
    return jax.shard_map(
        on_device,
        mesh=mesh,
        in_specs=(P("inp", "chan"), P()),
        out_specs=P("chan", "inp", None, None),
        check_vma=False,
    )
```

```python
import functools
import math

import jax
import jax.numpy as jnp
import numpy as np
from jax import lax
from jax.experimental import pallas as pl
from jax.experimental.pallas import tpu as pltpu
from jax.sharding import PartitionSpec as P

L = 2048
NCH = 512
TAPS = 4
LANES = 128
STEP = 4
COARSE = 16
EVERY = ("chan", "inp")


def filter_window():
    positions = np.arange(TAPS * L, dtype=np.float64)
    tapering = 0.5 - 0.5 * np.cos(2.0 * math.pi * positions / (TAPS * L))
    shape_sinc = np.sinc((positions - TAPS * L / 2.0) / L)
    return (shape_sinc * tapering).reshape(TAPS, L).astype(np.float32)


def twiddle_factors():
    samples = np.arange(L)[None, :]
    coarse = (COARSE * np.arange(NCH // COARSE)[:, None] * samples) % L
    rows = np.arange(2 * COARSE)[:, None]
    fine = ((rows // 2) * samples + (rows % 2) * (L // 4)) % L
    unit = 2.0 * math.pi / L
    tables = [np.cos(coarse * unit), np.sin(coarse * unit), np.cos(fine * unit), np.sin(fine * unit)]
    return [t.astype(np.float32) for t in tables]


def build_table(coarse_cos, coarse_sin, fine_cos, fine_sin, table):
    rows = 2 * COARSE

    def column(j, carry):
        lanes = pl.ds(pl.multiple_of(j * LANES, LANES), LANES)
        fc = fine_cos[:, lanes]
        fs = fine_sin[:, lanes]
        for a in range(NCH // COARSE):
            part = coarse_cos[a : a + 1, lanes] * fc - coarse_sin[a : a + 1, lanes] * fs
            table[a * rows : (a + 1) * rows, lanes] = part.astype(jnp.bfloat16)
        return carry

    lax.fori_loop(0, L // LANES, column, 0)


def filter_frames(window, current, following, filtered):
    width = current.shape[0]

    def column(j, carry):
        taps = [window[k : k + 1, pl.ds(pl.multiple_of(j * LANES, LANES), LANES)] for k in range(TAPS)]
        for r in range(0, width, 16):
            rows = slice(r, r + 16)
            frames = []
            for f in range(STEP + TAPS - 1):
                source, at = (current, f) if f < STEP else (following, f - STEP)
                lanes = pl.ds(pl.multiple_of(j * LANES + at * L, LANES), LANES)
                frames.append(source[rows, lanes].astype(jnp.float32))
            for f in range(STEP):
                total = frames[f] * taps[0]
                for k in range(1, TAPS):
                    total = total + frames[f + k] * taps[k]
                filtered[f * width + r : f * width + r + 16, pl.ds(pl.multiple_of(j * LANES, LANES), LANES)] = (
                    total.astype(jnp.bfloat16)
                )
        return carry

    lax.fori_loop(0, L // LANES, column, 0)


def transform(table, filtered, spectra):
    rows = 512

    def chunk(i, carry):
        at = pl.ds(pl.multiple_of(i * rows, rows), rows)
        product = lax.dot_general(
            table[at, :], filtered[...], (((1,), (1,)), ((), ())), preferred_element_type=jnp.float32
        )
        spectra[at, :] = product.astype(jnp.bfloat16)
        return carry

    lax.fori_loop(0, 2 * NCH // rows, chunk, 0)


def channelize_kernel(cc, cs, fc, fs, window, current, following, *refs):
    spectra, table, filtered = refs[-3:]

    @pl.when(pl.program_id(0) == 0)
    def _():
        build_table(cc, cs, fc, fs, table)

    filter_frames(window, current, following, filtered)
    transform(table, filtered, spectra)


def channelize(voltages):
    width, local_len = voltages.shape
    steps = local_len // (STEP * L)
    span = STEP * L
    halo = (TAPS - 1) * L
    devices = lax.axis_size("chan")
    halo_frames = lax.ppermute(voltages[:, :halo], "chan", [(i, i - 1) for i in range(1, devices)])
    window = jnp.asarray(filter_window())
    factors = [jnp.asarray(t) for t in twiddle_factors()]
    columns = STEP * width
    whole = lambda shape: pl.BlockSpec(shape, lambda *_: (0, 0), pipeline_mode=pl.Buffered(1))

    def call(name, first, count, following, earlier):
        given = [] if earlier is None else [earlier]
        if following is voltages:
            following_spec = pl.BlockSpec((width, span), lambda j: (0, first + j + 1))
        else:
            following_spec = whole((width, halo))
        return pl.pallas_call(
            channelize_kernel,
            name=name,
            grid=(count,),
            in_specs=[whole(t.shape) for t in factors]
            + [
                whole((TAPS, L)),
                pl.BlockSpec((width, span), lambda j: (0, first + j)),
                following_spec,
            ]
            + [pl.BlockSpec(memory_space=pl.ANY)] * len(given),
            out_specs=pl.BlockSpec((2 * NCH, columns), lambda j: (0, first + j)),
            out_shape=jax.ShapeDtypeStruct((2 * NCH, steps * columns), jnp.bfloat16),
            scratch_shapes=[pltpu.VMEM((2 * NCH, L), jnp.bfloat16), pltpu.VMEM((columns, L), jnp.bfloat16)],
            input_output_aliases={7: 0} if given else {},
            cost_estimate=pl.CostEstimate(flops=count * 10**9, bytes_accessed=6 * 2**20, transcendentals=0),
        )(*factors, window, voltages, following, *given)

    early = call("channelize_early", 0, steps - 1, voltages, None)
    return call("channelize_late", steps - 1, 1, halo_frames, early)


def gram_kernel(frame_total, slots, spectra, tiles, wide, lefts, rights, row_scale, col_scale, places):
    channel = pl.program_id(0)
    width = tiles.shape[1]
    blocks = lefts.shape[0] // width
    owners = blocks
    channels = spectra.shape[1] // 2
    per_owner = tiles.shape[0] // (owners * channels)
    times = spectra.shape[0] // blocks
    pieces = spectra.shape[2] // LANES
    parts = spectra.shape[1]
    depth = times * pieces

    @pl.when(channel == 0)
    def _():
        def unpack(b, carry):
            for t in range(times):
                rows = spectra[t * blocks + b].astype(jnp.float32)
                for p in range(pieces):
                    at = (t * pieces + p) * parts
                    wide[b, at : at + parts, :] = rows[:, p * LANES : (p + 1) * LANES]
            return carry

        lax.fori_loop(0, blocks, unpack, 0)

        def note(owner, carry):
            for k in range(per_owner):
                a, b = slots[owner * per_owner + k, 0], slots[owner * per_owner + k, 1]
                place = owner * (channels * per_owner) + k

                @pl.when(a >= 0)
                def _():
                    places[a * blocks + b] = place

                @pl.when(a < 0)
                def _():
                    for c in range(channels):
                        tiles[place + c * per_owner] = jnp.zeros((width, LANES), jnp.bfloat16)

            return carry

        lax.fori_loop(0, owners, note, 0)

    low = lax.broadcasted_iota(jnp.int32, (depth, LANES), 1) < width
    turn = lambda x: pltpu.roll(x, LANES // 2, 1)

    def scale(power):
        return lax.rsqrt(power / frame_total + 1e-6)

    def build(q, carry):
        pair = []
        for n in range(2):
            re = wide[2 * q + n, pl.ds(2 * channel, depth, stride=parts), :]
            im = wide[2 * q + n, pl.ds(2 * channel + 1, depth, stride=parts), :]
            re_turned, im_turned = turn(re), turn(im)
            pair.append((re, re_turned, im, im_turned))
            lanes = slice(n * LANES, (n + 1) * LANES)
            right = (
                jnp.where(low, re, -im_turned),
                jnp.where(low, re_turned, -im),
                jnp.where(low, im, re_turned),
                jnp.where(low, im_turned, re),
            )
            for k, part in enumerate(right):
                rights[q, k * depth : (k + 1) * depth, lanes] = part.astype(jnp.bfloat16)
            power = jnp.sum(re * re + im * im, axis=0, keepdims=True)
            col_scale[q, :, lanes] = scale(power + turn(power))
        x, y = pair
        flat = [jnp.where(low, x[k], y[k ^ 1]) for k in range(4)]
        flat = jnp.concatenate(flat, axis=0).astype(jnp.bfloat16).T
        rows = pl.ds(pl.multiple_of(q * LANES, LANES), LANES)
        lefts[rows, :] = flat
        flat = flat.astype(jnp.float32)
        row_scale[rows, :] = scale(jnp.sum(flat * flat, axis=1, keepdims=True)) / frame_total
        return carry

    lax.fori_loop(0, blocks // 2, build, 0)

    offset = channel * per_owner
    for q in range(blocks // 2):
        rows = (q + 1) * LANES
        product = jnp.dot(lefts[:rows, :], rights[q], preferred_element_type=jnp.float32)
        product = (product * row_scale[:rows, :] * col_scale[q]).astype(jnp.bfloat16)
        for n in range(2):
            for a in range(2 * q + n + 1):
                tile = product[a * width : (a + 1) * width, n * LANES : (n + 1) * LANES]
                tiles[places[a * blocks + 2 * q + n] + offset] = tile


def all_tiles(spectra, tile_table, blocks, width, frame_total):
    parts = spectra.shape[1]
    channels = parts // 2
    times = spectra.shape[0] // blocks
    depth = times * spectra.shape[2] // LANES
    per_owner = tile_table.shape[0] // blocks
    return pl.pallas_call(
        functools.partial(gram_kernel, float(frame_total)),
        name="gram",
        grid_spec=pltpu.PrefetchScalarGridSpec(
            num_scalar_prefetch=1,
            grid=(channels,),
            in_specs=[pl.BlockSpec(spectra.shape, lambda c, s: (0, 0, 0), pipeline_mode=pl.Buffered(1))],
            out_specs=pl.BlockSpec(memory_space=pltpu.VMEM),
            scratch_shapes=[
                pltpu.VMEM((blocks, depth * parts, LANES), jnp.float32),
                pltpu.VMEM((blocks * width, 4 * depth), jnp.bfloat16),
                pltpu.VMEM((blocks // 2, 4 * depth, 2 * LANES), jnp.bfloat16),
                pltpu.VMEM((blocks * width, 1), jnp.float32),
                pltpu.VMEM((blocks // 2, 1, 2 * LANES), jnp.float32),
                pltpu.SMEM((blocks * blocks,), jnp.int32),
            ],
        ),
        out_shape=jax.ShapeDtypeStruct((blocks * channels * per_owner, width, 2 * width), jnp.bfloat16),
        compiler_params=pltpu.CompilerParams(vmem_limit_bytes=32 * 2**20),
        cost_estimate=pl.CostEstimate(flops=3 * 10**9, bytes_accessed=12 * 2**20, transcendentals=0),
    )(tile_table, spectra)


def widen_kernel(tiles, out):
    out[...] = tiles[...].astype(jnp.float32)


def widen(tiles):
    sources, channels, per_owner, width, lanes = tiles.shape
    block = (1, channels, per_owner, width, lanes)
    at = lambda d: (d, 0, 0, 0, 0)
    return pl.pallas_call(
        widen_kernel,
        name="widen",
        grid=(sources,),
        in_specs=[pl.BlockSpec(block, at)],
        out_specs=pl.BlockSpec(block, at),
        out_shape=jax.ShapeDtypeStruct(tiles.shape, jnp.float32),
        compiler_params=pltpu.CompilerParams(vmem_limit_bytes=24 * 2**20),
        cost_estimate=pl.CostEstimate(flops=0, bytes_accessed=28 * 2**20, transcendentals=0),
    )(tiles)


def on_device(voltages, tile_table):
    width, local_len = voltages.shape
    blocks = lax.axis_size("inp")
    devices = blocks * lax.axis_size("chan")
    frame_total = local_len // L * lax.axis_size("chan")
    spectra = channelize(voltages)
    spectra = spectra.reshape(devices, 2 * NCH // devices, spectra.shape[1])
    turned = lax.all_to_all(spectra, EVERY, 0, 0, tiled=True)
    tiles = all_tiles(turned, tile_table, blocks, width, frame_total)
    tiles = tiles.reshape(blocks, -1, tile_table.shape[0] // blocks, *tiles.shape[1:])
    out = widen(lax.all_to_all(tiles, "inp", 0, 0, tiled=True))
    return out.reshape(-1, *out.shape[2:])


def solution(mesh):
    return jax.shard_map(
        on_device,
        mesh=mesh,
        in_specs=(P("inp", "chan"), P()),
        out_specs=P("chan", "inp", None, None),
        check_vma=False,
    )
```

```python
import functools
import math

import jax
import jax.numpy as jnp
import numpy as np
from jax import lax
from jax.experimental import pallas as pl
from jax.experimental.pallas import tpu as pltpu
from jax.sharding import PartitionSpec as P

L = 2048
NCH = 512
TAPS = 4
LANES = 128
STEP = 4
COARSE = 16
EVERY = ("chan", "inp")


def filter_window():
    positions = np.arange(TAPS * L, dtype=np.float64)
    tapering = 0.5 - 0.5 * np.cos(2.0 * math.pi * positions / (TAPS * L))
    shape_sinc = np.sinc((positions - TAPS * L / 2.0) / L)
    return (shape_sinc * tapering).reshape(TAPS, L).astype(np.float32)


def twiddle_factors():
    unit = 2.0 * math.pi / L
    coarse = (COARSE * np.arange(NCH // COARSE)[:, None] * np.arange(L // COARSE)[None, :]) % L
    rows = np.arange(2 * COARSE)[:, None]
    fine = ((rows // 2) * np.arange(L // 2)[None, :] + (rows % 2) * (L // 4)) % L
    both = lambda phases: np.concatenate([np.cos(phases * unit), np.sin(phases * unit)]).astype(np.float32)
    return both(coarse), both(fine)


def build_table(coarse, fine, table):
    rows = 2 * COARSE
    groups = NCH // COARSE
    channel = lax.broadcasted_iota(jnp.int32, (rows, LANES), 0) // 2
    later = jnp.where(channel % 2 == 0, 1.0, -1.0).astype(jnp.float32)

    def column(j, carry):
        lanes = pl.ds(pl.multiple_of(j * LANES, LANES), LANES)
        lanes_later = pl.ds(pl.multiple_of(j * LANES + L // 2, LANES), LANES)
        fine_cos, fine_sin = fine[:rows, lanes], fine[rows:, lanes]
        for a in range(groups):
            part = coarse[a : a + 1, :] * fine_cos - coarse[groups + a : groups + a + 1, :] * fine_sin
            table[a * rows : (a + 1) * rows, lanes] = part.astype(jnp.bfloat16)
            table[a * rows : (a + 1) * rows, lanes_later] = (part * later).astype(jnp.bfloat16)
        return carry

    lax.fori_loop(0, L // 2 // LANES, column, 0)


def filter_column(window, frames, filtered, j):
    width = frames[0][0].shape[0]
    at = pl.ds(pl.multiple_of(j * LANES, LANES), LANES)
    taps = [window[k : k + 1, at] for k in range(TAPS)]
    for r in range(0, width, 16):
        rows = slice(r, r + 16)
        samples = [
            source[rows, pl.ds(pl.multiple_of(first + j * LANES, LANES), LANES)].astype(jnp.float32)
            for source, first in frames
        ]
        for f in range(STEP):
            total = samples[f] * taps[0]
            for k in range(1, TAPS):
                total = total + samples[f + k] * taps[k]
            filtered[f * width + r : f * width + r + 16, at] = total.astype(jnp.bfloat16)


def filter_frames(window, frames, filtered):
    def column(j, carry):
        filter_column(window, frames, filtered, j)
        return carry

    lax.fori_loop(0, L // LANES, column, 0)


def transform(table, filtered, spectra, beside=None):
    rows = 512
    chunks = 2 * NCH // rows
    share = L // LANES // chunks

    def chunk(i, carry):
        at = pl.ds(pl.multiple_of(i * rows, rows), rows)
        product = lax.dot_general(
            table[at, :], filtered[...], (((1,), (1,)), ((), ())), preferred_element_type=jnp.float32
        )
        spectra[at, :] = product.astype(jnp.bfloat16)
        if beside is not None:
            for j in range(share):
                beside(i * share + j)
        return carry

    lax.fori_loop(0, chunks, chunk, 0)


def early_kernel(
    coarse_hbm, fine_hbm, window_hbm, voltages, spectra, table, last, window, coarse, fine, head, even, odd, parts, sems, out_sems
):
    span = STEP * L
    width = even.shape[0]
    steps = spectra.shape[1] // width
    small = [(coarse_hbm, coarse), (fine_hbm, fine), (window_hbm, window)]
    loads = [pltpu.make_async_copy(source, target, sems.at[n]) for n, (source, target) in enumerate(small)]
    copies = []
    for n in range(steps):
        target = last if n == steps - 1 else head.at[:, n * span : (n + 1) * span]
        source = voltages.at[:, n * span : (n + 1) * span]
        copies.append(pltpu.make_async_copy(source, target, sems.at[len(small) + n]))
    for copy in loads + copies:
        copy.start()
    for copy in loads:
        copy.wait()
    build_table(coarse, fine, table)
    places = [(head, f * L) for f in range((steps - 1) * STEP)] + [(last, f * L) for f in range(STEP)]
    frames = lambda n: places[n * STEP : (n + 1) * STEP + TAPS - 1]
    copies[0].wait()
    copies[1].wait()
    filtered = [even, odd]
    filter_frames(window, frames(0), even)
    outs = []
    for n in range(steps - 1):
        beside = None
        if n < steps - 2:
            copies[n + 2].wait()
            beside = lambda j, n=n: filter_column(window, frames(n + 1), filtered[(n + 1) % 2], j)
        transform(table, filtered[n % 2], parts.at[n], beside)
        columns = spectra.at[:, n * width : (n + 1) * width]
        outs.append(pltpu.make_async_copy(parts.at[n], columns, out_sems.at[n]))
        outs[n].start()
    for copy in outs:
        copy.wait()


def late_kernel(table, window, last, following, earlier, spectra, filtered):
    del earlier
    frames = [(last, f * L) for f in range(STEP)] + [(following, f * L) for f in range(TAPS - 1)]
    filter_frames(window, frames, filtered)
    transform(table, filtered, spectra)


def in_hbm(array):
    return pltpu.with_memory_space_constraint(array, pltpu.HBM)


def channelize(voltages):
    width, local_len = voltages.shape
    steps = local_len // (STEP * L)
    span = STEP * L
    halo = (TAPS - 1) * L
    devices = lax.axis_size("chan")
    following = lax.ppermute(voltages[:, :halo], "chan", [(i, i - 1) for i in range(1, devices)])
    constants = [*twiddle_factors(), filter_window()]
    columns = STEP * width
    here = pl.BlockSpec(memory_space=pltpu.VMEM)
    hbm = pl.BlockSpec(memory_space=pltpu.HBM)
    spectra_shape = jax.ShapeDtypeStruct((2 * NCH, steps * columns), jnp.bfloat16)
    filtered = pltpu.VMEM((columns, L), jnp.bfloat16)
    early, table, last, window = pl.pallas_call(
        early_kernel,
        name="channelize_early",
        in_specs=[hbm] * 4,
        out_specs=[hbm, here, here, here],
        out_shape=[
            spectra_shape,
            jax.ShapeDtypeStruct((2 * NCH, L), jnp.bfloat16),
            jax.ShapeDtypeStruct((width, span), jnp.bfloat16),
            jax.ShapeDtypeStruct((TAPS, L), jnp.float32),
        ],
        scratch_shapes=[
            pltpu.VMEM(constants[0].shape, jnp.float32),
            pltpu.VMEM(constants[1].shape, jnp.float32),
            pltpu.VMEM((width, local_len - span), jnp.bfloat16),
            filtered,
            filtered,
            pltpu.VMEM((steps - 1, 2 * NCH, columns), jnp.bfloat16),
            pltpu.SemaphoreType.DMA((3 + steps,)),
            pltpu.SemaphoreType.DMA((steps - 1,)),
        ],
        compiler_params=pltpu.CompilerParams(vmem_limit_bytes=24 * 2**20),
        cost_estimate=pl.CostEstimate(flops=3 * 10**9, bytes_accessed=12 * 2**20, transcendentals=0),
    )(*(in_hbm(jnp.asarray(t)) for t in constants), in_hbm(voltages))
    return pl.pallas_call(
        late_kernel,
        name="channelize_late",
        grid=(1,),
        in_specs=[here] * 4 + [pl.BlockSpec(memory_space=pl.ANY)],
        out_specs=pl.BlockSpec((2 * NCH, columns), lambda j: (0, steps - 1)),
        out_shape=spectra_shape,
        scratch_shapes=[filtered],
        input_output_aliases={4: 0},
        compiler_params=pltpu.CompilerParams(vmem_limit_bytes=24 * 2**20),
        cost_estimate=pl.CostEstimate(flops=10**9, bytes_accessed=6 * 2**20, transcendentals=0),
    )(table, window, last, following, early)


def places_kernel(channels, slots, places):
    blocks = places.shape[1]
    per_owner = slots.shape[0] // blocks

    def owner_slots(owner, empty):
        for k in range(per_owner):
            a, b = slots[owner * per_owner + k, 0], slots[owner * per_owner + k, 1]
            present = a >= 0
            row = jnp.where(present, a, blocks + 1)
            column = jnp.where(present, b, empty)
            places[row, column] = owner * (channels * per_owner) + k
            empty = empty + jnp.where(present, 0, 1)
        return empty

    places[blocks, 0] = lax.fori_loop(0, blocks, owner_slots, 0)


def slot_places(tile_table, blocks, channels):
    return pl.pallas_call(
        functools.partial(places_kernel, channels),
        name="places",
        in_specs=[pl.BlockSpec(memory_space=pltpu.SMEM)],
        out_specs=pl.BlockSpec(memory_space=pltpu.SMEM),
        out_shape=jax.ShapeDtypeStruct((blocks + 2, blocks), jnp.int32),
        cost_estimate=pl.CostEstimate(flops=10**6, bytes_accessed=2**12, transcendentals=0),
    )(tile_table)


def gram_kernel(frame_total, places, spectra, tiles, wide, lefts, rights, row_scale, col_scale):
    channel = pl.program_id(0)
    width = tiles.shape[1]
    blocks = lefts.shape[0] // width
    owners = blocks
    channels = spectra.shape[1] // 2
    per_owner = tiles.shape[0] // (owners * channels)
    times = spectra.shape[0] // blocks
    pieces = spectra.shape[2] // LANES
    parts = spectra.shape[1]
    depth = times * pieces

    @pl.when(channel == 0)
    def _():
        def unpack(b, carry):
            for t in range(times):
                rows = spectra[t * blocks + b].astype(jnp.float32)
                for p in range(pieces):
                    at = (t * pieces + p) * parts
                    wide[b, at : at + parts, :] = rows[:, p * LANES : (p + 1) * LANES]
            return carry

        lax.fori_loop(0, blocks, unpack, 0)

        def clear(n, carry):
            for c in range(channels):
                tiles[places[blocks + 1, n] + c * per_owner] = jnp.zeros((width, LANES), jnp.bfloat16)
            return carry

        lax.fori_loop(0, places[blocks, 0], clear, 0)

    low = lax.broadcasted_iota(jnp.int32, (depth, LANES), 1) < width
    turn = lambda x: pltpu.roll(x, LANES // 2, 1)

    def scale(power):
        return lax.rsqrt(power / frame_total + 1e-6)

    def build(q, carry):
        pair = []
        for n in range(2):
            re = wide[2 * q + n, pl.ds(2 * channel, depth, stride=parts), :]
            im = wide[2 * q + n, pl.ds(2 * channel + 1, depth, stride=parts), :]
            re_turned, im_turned = turn(re), turn(im)
            pair.append((re, re_turned, im, im_turned))
            lanes = slice(n * LANES, (n + 1) * LANES)
            right = (
                jnp.where(low, re, -im_turned),
                jnp.where(low, re_turned, -im),
                jnp.where(low, im, re_turned),
                jnp.where(low, im_turned, re),
            )
            for k, part in enumerate(right):
                rights[q, k * depth : (k + 1) * depth, lanes] = part.astype(jnp.bfloat16)
            power = jnp.sum(re * re + im * im, axis=0, keepdims=True)
            col_scale[q, :, lanes] = scale(power + turn(power))
        x, y = pair
        flat = [jnp.where(low, x[k], y[k ^ 1]) for k in range(4)]
        flat = jnp.concatenate(flat, axis=0).astype(jnp.bfloat16).T
        rows = pl.ds(pl.multiple_of(q * LANES, LANES), LANES)
        lefts[rows, :] = flat
        flat = flat.astype(jnp.float32)
        row_scale[rows, :] = scale(jnp.sum(flat * flat, axis=1, keepdims=True)) / frame_total
        return carry

    lax.fori_loop(0, blocks // 2, build, 0, unroll=2)

    offset = channel * per_owner
    for q in range(blocks // 2):
        rows = (q + 1) * LANES
        product = jnp.dot(lefts[:rows, :], rights[q], preferred_element_type=jnp.float32)
        product = (product * row_scale[:rows, :] * col_scale[q]).astype(jnp.bfloat16)
        for n in range(2):
            for a in range(2 * q + n + 1):
                tile = product[a * width : (a + 1) * width, n * LANES : (n + 1) * LANES]
                tiles[places[a, 2 * q + n] + offset] = tile


def all_tiles(spectra, tile_table, blocks, width, frame_total):
    parts = spectra.shape[1]
    channels = parts // 2
    times = spectra.shape[0] // blocks
    depth = times * spectra.shape[2] // LANES
    per_owner = tile_table.shape[0] // blocks
    return pl.pallas_call(
        functools.partial(gram_kernel, float(frame_total)),
        name="gram",
        grid_spec=pltpu.PrefetchScalarGridSpec(
            num_scalar_prefetch=1,
            grid=(channels,),
            in_specs=[pl.BlockSpec(spectra.shape, lambda c, s: (0, 0, 0), pipeline_mode=pl.Buffered(1))],
            out_specs=pl.BlockSpec(memory_space=pltpu.VMEM),
            scratch_shapes=[
                pltpu.VMEM((blocks, depth * parts, LANES), jnp.float32),
                pltpu.VMEM((blocks * width, 4 * depth), jnp.bfloat16),
                pltpu.VMEM((blocks // 2, 4 * depth, 2 * LANES), jnp.bfloat16),
                pltpu.VMEM((blocks * width, 1), jnp.float32),
                pltpu.VMEM((blocks // 2, 1, 2 * LANES), jnp.float32),
            ],
        ),
        out_shape=jax.ShapeDtypeStruct((blocks * channels * per_owner, width, 2 * width), jnp.bfloat16),
        compiler_params=pltpu.CompilerParams(vmem_limit_bytes=32 * 2**20),
        cost_estimate=pl.CostEstimate(flops=3 * 10**9, bytes_accessed=12 * 2**20, transcendentals=0),
    )(in_hbm(slot_places(tile_table, blocks, channels)), spectra)


def widen_kernel(tiles, out):
    out[...] = tiles[...].astype(jnp.float32)


def widen(tiles):
    sources, channels, per_owner, width, lanes = tiles.shape
    block = (sources // 8, channels, per_owner, width, lanes)
    at = lambda d: (d, 0, 0, 0, 0)
    return pl.pallas_call(
        widen_kernel,
        name="widen",
        grid=(8,),
        in_specs=[pl.BlockSpec(block, at)],
        out_specs=pl.BlockSpec(block, at),
        out_shape=jax.ShapeDtypeStruct(tiles.shape, jnp.float32),
        compiler_params=pltpu.CompilerParams(vmem_limit_bytes=24 * 2**20),
        cost_estimate=pl.CostEstimate(flops=0, bytes_accessed=28 * 2**20, transcendentals=0),
    )(tiles)


def on_device(voltages, tile_table):
    width, local_len = voltages.shape
    blocks = lax.axis_size("inp")
    devices = blocks * lax.axis_size("chan")
    frame_total = local_len // L * lax.axis_size("chan")
    spectra = channelize(voltages)
    spectra = spectra.reshape(devices, 2 * NCH // devices, spectra.shape[1])
    turned = lax.all_to_all(spectra, EVERY, 0, 0, tiled=True)
    tiles = all_tiles(turned, tile_table, blocks, width, frame_total)
    tiles = tiles.reshape(blocks, -1, tile_table.shape[0] // blocks, *tiles.shape[1:])
    out = widen(lax.all_to_all(tiles, "inp", 0, 0, tiled=True))
    return out.reshape(-1, *out.shape[2:])


def solution(mesh):
    return jax.shard_map(
        on_device,
        mesh=mesh,
        in_specs=(P("inp", "chan"), P()),
        out_specs=P("chan", "inp", None, None),
        check_vma=False,
    )
```

```python
import functools
import math

import jax
import jax.numpy as jnp
import numpy as np
from jax import lax
from jax.experimental import pallas as pl
from jax.experimental.pallas import tpu as pltpu
from jax.sharding import PartitionSpec as P

L = 2048
NCH = 512
TAPS = 4
LANES = 128
STEP = 4
COARSE = 16
EVERY = ("chan", "inp")


def filter_window():
    positions = np.arange(TAPS * L, dtype=np.float64)
    tapering = 0.5 - 0.5 * np.cos(2.0 * math.pi * positions / (TAPS * L))
    shape_sinc = np.sinc((positions - TAPS * L / 2.0) / L)
    return (shape_sinc * tapering).reshape(TAPS, L).astype(np.float32)


def twiddle_factors():
    unit = 2.0 * math.pi / L
    coarse = (COARSE * np.arange(NCH // COARSE)[:, None] * np.arange(L // COARSE)[None, :]) % L
    rows = np.arange(2 * COARSE)[:, None]
    fine = ((rows // 2) * np.arange(L // 2)[None, :] + (rows % 2) * (L // 4)) % L
    both = lambda phases: np.concatenate([np.cos(phases * unit), np.sin(phases * unit)]).astype(np.float32)
    return both(coarse), both(fine)


def build_table(coarse, fine, table):
    rows = 2 * COARSE
    groups = NCH // COARSE
    channel = lax.broadcasted_iota(jnp.int32, (rows, LANES), 0) // 2
    later = jnp.where(channel % 2 == 0, 1.0, -1.0).astype(jnp.float32)

    def column(j, carry):
        lanes = pl.ds(pl.multiple_of(j * LANES, LANES), LANES)
        lanes_later = pl.ds(pl.multiple_of(j * LANES + L // 2, LANES), LANES)
        fine_cos, fine_sin = fine[:rows, lanes], fine[rows:, lanes]
        for a in range(groups):
            part = coarse[a : a + 1, :] * fine_cos - coarse[groups + a : groups + a + 1, :] * fine_sin
            table[a * rows : (a + 1) * rows, lanes] = part.astype(jnp.bfloat16)
            table[a * rows : (a + 1) * rows, lanes_later] = (part * later).astype(jnp.bfloat16)
        return carry

    lax.fori_loop(0, L // 2 // LANES, column, 0)


def filter_column(window, frames, filtered, j):
    width = frames[0][0].shape[0]
    at = pl.ds(pl.multiple_of(j * LANES, LANES), LANES)
    taps = [window[k : k + 1, at] for k in range(TAPS)]
    for r in range(0, width, 16):
        rows = slice(r, r + 16)
        samples = [
            source[rows, pl.ds(pl.multiple_of(first + j * LANES, LANES), LANES)].astype(jnp.float32)
            for source, first in frames
        ]
        for f in range(STEP):
            total = samples[f] * taps[0]
            for k in range(1, TAPS):
                total = total + samples[f + k] * taps[k]
            filtered[f * width + r : f * width + r + 16, at] = total.astype(jnp.bfloat16)


def filter_frames(window, frames, filtered, beside=None, start=0):
    def column(j, carry):
        filter_column(window, frames, filtered, j)
        return carry if beside is None else beside(j, carry)

    return lax.fori_loop(0, L // LANES, column, start)


def note_places(slots, places, channels, owner, empty):
    blocks = L // LANES
    per_owner = slots.shape[1] // blocks
    for k in range(per_owner):
        a, b = slots[0, owner * per_owner + k], slots[1, owner * per_owner + k]
        place = owner * (channels * per_owner) + k
        present = a >= 0
        places[jnp.where(present, a * blocks + b, blocks * blocks + empty)] = place
        empty = empty + jnp.where(present, 0, 1)
    return empty


def transform(table, filtered, spectra, columns, beside=None):
    rows = 512
    chunks = 2 * NCH // rows
    share = L // LANES // chunks

    def chunk(i, carry):
        at = pl.ds(pl.multiple_of(i * rows, rows), rows)
        product = lax.dot_general(
            table[at, :], filtered[...], (((1,), (1,)), ((), ())), preferred_element_type=jnp.float32
        )
        spectra[at, columns] = product.astype(jnp.bfloat16)
        if beside is not None:
            for j in range(share):
                beside(i * share + j)
        return carry

    lax.fori_loop(0, chunks, chunk, 0)


def early_kernel(
    channels, coarse_hbm, fine_hbm, window_hbm, voltages, slots, spectra, table, last, window, places,
    coarse, fine, head, even, odd, sems,
):
    span = STEP * L
    width = even.shape[0]
    steps = spectra.shape[1] // width
    small = [(coarse_hbm, coarse), (fine_hbm, fine), (window_hbm, window)]
    loads = [pltpu.make_async_copy(source, target, sems.at[n]) for n, (source, target) in enumerate(small)]
    copies = []
    for n in range(steps):
        target = last if n == steps - 1 else head.at[:, n * span : (n + 1) * span]
        source = voltages.at[:, n * span : (n + 1) * span]
        copies.append(pltpu.make_async_copy(source, target, sems.at[len(small) + n]))
    for copy in loads + copies:
        copy.start()
    for copy in loads:
        copy.wait()
    build_table(coarse, fine, table)
    samples = [(head, f * L) for f in range((steps - 1) * STEP)] + [(last, f * L) for f in range(STEP)]
    frames = lambda n: samples[n * STEP : (n + 1) * STEP + TAPS - 1]
    copies[0].wait()
    copies[1].wait()
    filtered = [even, odd]
    note = lambda j, empty: note_places(slots, places, channels, j, empty)
    places[places.shape[0] - 1] = filter_frames(window, frames(0), even, note, 0)
    for n in range(steps - 1):
        beside = None
        if n < steps - 2:
            copies[n + 2].wait()
            beside = lambda j, n=n: filter_column(window, frames(n + 1), filtered[(n + 1) % 2], j)
        transform(table, filtered[n % 2], spectra, slice(n * width, (n + 1) * width), beside)


def late_kernel(table, window, last, following, earlier, spectra, filtered):
    del earlier
    frames = [(last, f * L) for f in range(STEP)] + [(following, f * L) for f in range(TAPS - 1)]
    filter_frames(window, frames, filtered)
    first = spectra.shape[1] - filtered.shape[0]
    transform(table, filtered, spectra, slice(first, spectra.shape[1]))


def in_hbm(array):
    return pltpu.with_memory_space_constraint(array, pltpu.HBM)


def channelize(voltages, tile_table, blocks, channels):
    width, local_len = voltages.shape
    steps = local_len // (STEP * L)
    span = STEP * L
    halo = (TAPS - 1) * L
    devices = lax.axis_size("chan")
    following = lax.ppermute(voltages[:, :halo], "chan", [(i, i - 1) for i in range(1, devices)])
    constants = [*twiddle_factors(), filter_window()]
    assert blocks == L // LANES
    columns = STEP * width
    here = pl.BlockSpec(memory_space=pltpu.VMEM)
    hbm = pl.BlockSpec(memory_space=pltpu.HBM)
    spectra_shape = jax.ShapeDtypeStruct((2 * NCH, steps * columns), jnp.bfloat16)
    filtered = pltpu.VMEM((columns, L), jnp.bfloat16)
    smem = pl.BlockSpec(memory_space=pltpu.SMEM)
    early, table, last, window, places = pl.pallas_call(
        functools.partial(early_kernel, channels),
        name="channelize_early",
        in_specs=[hbm] * 4 + [smem],
        out_specs=[here] * 4 + [smem],
        out_shape=[
            spectra_shape,
            jax.ShapeDtypeStruct((2 * NCH, L), jnp.bfloat16),
            jax.ShapeDtypeStruct((width, span), jnp.bfloat16),
            jax.ShapeDtypeStruct((TAPS, L), jnp.float32),
            jax.ShapeDtypeStruct((blocks * blocks + tile_table.shape[0] + 1,), jnp.int32),
        ],
        scratch_shapes=[
            pltpu.VMEM(constants[0].shape, jnp.float32),
            pltpu.VMEM(constants[1].shape, jnp.float32),
            pltpu.VMEM((width, local_len - span), jnp.bfloat16),
            filtered,
            filtered,
            pltpu.SemaphoreType.DMA((3 + steps,)),
        ],
        compiler_params=pltpu.CompilerParams(vmem_limit_bytes=24 * 2**20),
        cost_estimate=pl.CostEstimate(flops=3 * 10**9, bytes_accessed=12 * 2**20, transcendentals=0),
    )(*(in_hbm(jnp.asarray(t)) for t in constants), in_hbm(voltages), tile_table.T)
    spectra = pl.pallas_call(
        late_kernel,
        name="channelize_late",
        in_specs=[here] * 5,
        out_specs=here,
        out_shape=spectra_shape,
        scratch_shapes=[filtered],
        input_output_aliases={4: 0},
        compiler_params=pltpu.CompilerParams(vmem_limit_bytes=24 * 2**20),
        cost_estimate=pl.CostEstimate(flops=10**9, bytes_accessed=6 * 2**20, transcendentals=0),
    )(table, window, last, following, early)
    return spectra, places


def gram_kernel(frame_total, places, spectra, tiles, wide, lefts, rights, row_scale, col_scale):
    channel = pl.program_id(0)
    width = tiles.shape[1]
    blocks = lefts.shape[0] // width
    owners = blocks
    channels = spectra.shape[1] // 2
    per_owner = tiles.shape[0] // (owners * channels)
    times = spectra.shape[0] // blocks
    pieces = spectra.shape[2] // LANES
    parts = spectra.shape[1]
    depth = times * pieces

    @pl.when(channel == 0)
    def _():
        def unpack(b, carry):
            for t in range(times):
                rows = spectra[t * blocks + b].astype(jnp.float32)
                for p in range(pieces):
                    at = (t * pieces + p) * parts
                    wide[b, at : at + parts, :] = rows[:, p * LANES : (p + 1) * LANES]
            return carry

        lax.fori_loop(0, blocks, unpack, 0)

        def clear(n, carry):
            for c in range(channels):
                tiles[places[blocks * blocks + n] + c * per_owner] = jnp.zeros((width, LANES), jnp.bfloat16)
            return carry

        lax.fori_loop(0, places[places.shape[0] - 1], clear, 0)

    low = lax.broadcasted_iota(jnp.int32, (depth, LANES), 1) < width
    turn = lambda x: pltpu.roll(x, LANES // 2, 1)

    def scale(power):
        return lax.rsqrt(power / frame_total + 1e-6)

    def build(q, carry):
        pair = []
        for n in range(2):
            re = wide[2 * q + n, pl.ds(2 * channel, depth, stride=parts), :]
            im = wide[2 * q + n, pl.ds(2 * channel + 1, depth, stride=parts), :]
            power = jnp.sum(re * re + im * im, axis=0, keepdims=True)
            re, im = re.astype(jnp.bfloat16), im.astype(jnp.bfloat16)
            re_turned, im_turned = turn(re), turn(im)
            pair.append((re, re_turned, im, im_turned))
            lanes = slice(n * LANES, (n + 1) * LANES)
            right = (
                jnp.where(low, re, -im_turned),
                jnp.where(low, re_turned, -im),
                jnp.where(low, im, re_turned),
                jnp.where(low, im_turned, re),
            )
            for k, part in enumerate(right):
                rights[q, k * depth : (k + 1) * depth, lanes] = part
            col_scale[q, :, lanes] = scale(power + turn(power))
        x, y = pair
        flat = [jnp.where(low, x[k], y[k ^ 1]) for k in range(4)]
        flat = jnp.concatenate(flat, axis=0).T
        rows = pl.ds(pl.multiple_of(q * LANES, LANES), LANES)
        lefts[rows, :] = flat
        flat = flat.astype(jnp.float32)
        row_scale[rows, :] = scale(jnp.sum(flat * flat, axis=1, keepdims=True)) / frame_total
        return carry

    lax.fori_loop(0, blocks // 2, build, 0, unroll=2)

    offset = channel * per_owner
    for q in range(blocks // 2):
        rows = (q + 1) * LANES
        product = jnp.dot(lefts[:rows, :], rights[q], preferred_element_type=jnp.float32)
        product = (product * row_scale[:rows, :] * col_scale[q]).astype(jnp.bfloat16)
        for n in range(2):
            for a in range(2 * q + n + 1):
                tile = product[a * width : (a + 1) * width, n * LANES : (n + 1) * LANES]
                tiles[places[a * blocks + 2 * q + n] + offset] = tile


def all_tiles(spectra, places, per_owner, blocks, width, frame_total):
    parts = spectra.shape[1]
    channels = parts // 2
    times = spectra.shape[0] // blocks
    depth = times * spectra.shape[2] // LANES
    return pl.pallas_call(
        functools.partial(gram_kernel, float(frame_total)),
        name="gram",
        grid_spec=pltpu.PrefetchScalarGridSpec(
            num_scalar_prefetch=1,
            grid=(channels,),
            in_specs=[pl.BlockSpec(spectra.shape, lambda c, s: (0, 0, 0), pipeline_mode=pl.Buffered(1))],
            out_specs=pl.BlockSpec(memory_space=pltpu.VMEM),
            scratch_shapes=[
                pltpu.VMEM((blocks, depth * parts, LANES), jnp.float32),
                pltpu.VMEM((blocks * width, 4 * depth), jnp.bfloat16),
                pltpu.VMEM((blocks // 2, 4 * depth, 2 * LANES), jnp.bfloat16),
                pltpu.VMEM((blocks * width, 1), jnp.float32),
                pltpu.VMEM((blocks // 2, 1, 2 * LANES), jnp.float32),
            ],
        ),
        out_shape=jax.ShapeDtypeStruct((blocks * channels * per_owner, width, 2 * width), jnp.bfloat16),
        compiler_params=pltpu.CompilerParams(vmem_limit_bytes=32 * 2**20),
        cost_estimate=pl.CostEstimate(flops=3 * 10**9, bytes_accessed=12 * 2**20, transcendentals=0),
    )(places, spectra)


def widen_kernel(tiles, out):
    out[...] = tiles[...].astype(jnp.float32)


def widen(tiles):
    sources, channels, per_owner, width, lanes = tiles.shape
    block = (sources // 8, channels, per_owner, width, lanes)
    at = lambda d: (d, 0, 0, 0, 0)
    return pl.pallas_call(
        widen_kernel,
        name="widen",
        grid=(8,),
        in_specs=[pl.BlockSpec(block, at)],
        out_specs=pl.BlockSpec(block, at),
        out_shape=jax.ShapeDtypeStruct(tiles.shape, jnp.float32),
        compiler_params=pltpu.CompilerParams(vmem_limit_bytes=24 * 2**20),
        cost_estimate=pl.CostEstimate(flops=0, bytes_accessed=28 * 2**20, transcendentals=0),
    )(tiles)


def on_device(voltages, tile_table):
    width, local_len = voltages.shape
    blocks = lax.axis_size("inp")
    devices = blocks * lax.axis_size("chan")
    frame_total = local_len // L * lax.axis_size("chan")
    channels = NCH // devices
    per_owner = tile_table.shape[0] // blocks
    spectra, places = channelize(voltages, tile_table, blocks, channels)
    spectra = spectra.reshape(devices, 2 * channels, spectra.shape[1])
    turned = lax.all_to_all(spectra, EVERY, 0, 0, tiled=True)
    tiles = all_tiles(turned, places, per_owner, blocks, width, frame_total)
    tiles = tiles.reshape(blocks, channels, per_owner, *tiles.shape[1:])
    out = widen(lax.all_to_all(tiles, "inp", 0, 0, tiled=True))
    return out.reshape(-1, *out.shape[2:])


def solution(mesh):
    return jax.shard_map(
        on_device,
        mesh=mesh,
        in_specs=(P("inp", "chan"), P()),
        out_specs=P("chan", "inp", None, None),
        check_vma=False,
    )
```

```python
import functools
import math

import jax
import jax.numpy as jnp
import numpy as np
from jax import lax
from jax.experimental import pallas as pl
from jax.experimental.pallas import tpu as pltpu
from jax.sharding import PartitionSpec as P

L = 2048
NCH = 512
TAPS = 4
LANES = 128
STEP = 4
COARSE = 16
EVERY = ("chan", "inp")


def filter_window():
    positions = np.arange(TAPS * L, dtype=np.float64)
    tapering = 0.5 - 0.5 * np.cos(2.0 * math.pi * positions / (TAPS * L))
    shape_sinc = np.sinc((positions - TAPS * L / 2.0) / L)
    return (shape_sinc * tapering).reshape(TAPS, L).astype(np.float32)


def twiddle_factors():
    unit = 2.0 * math.pi / L
    coarse = (COARSE * np.arange(NCH // COARSE)[:, None] * np.arange(L // COARSE)[None, :]) % L
    rows = np.arange(2 * COARSE)[:, None]
    fine = ((rows // 2) * np.arange(L // 2)[None, :] + (rows % 2) * (L // 4)) % L
    both = lambda phases: np.concatenate([np.cos(phases * unit), np.sin(phases * unit)]).astype(np.float32)
    return both(coarse), both(fine)


def build_table(coarse, fine, table):
    rows = 2 * COARSE
    groups = NCH // COARSE
    channel = lax.broadcasted_iota(jnp.int32, (rows, LANES), 0) // 2
    later = jnp.where(channel % 2 == 0, 1.0, -1.0).astype(jnp.float32)

    def column(j, carry):
        lanes = pl.ds(pl.multiple_of(j * LANES, LANES), LANES)
        lanes_later = pl.ds(pl.multiple_of(j * LANES + L // 2, LANES), LANES)
        fine_cos, fine_sin = fine[:rows, lanes], fine[rows:, lanes]
        for a in range(groups):
            part = coarse[a : a + 1, :] * fine_cos - coarse[groups + a : groups + a + 1, :] * fine_sin
            table[a * rows : (a + 1) * rows, lanes] = part.astype(jnp.bfloat16)
            table[a * rows : (a + 1) * rows, lanes_later] = (part * later).astype(jnp.bfloat16)
        return carry

    lax.fori_loop(0, L // 2 // LANES, column, 0)


def filter_column(window, frames, filtered, j):
    width = frames[0][0].shape[0]
    at = pl.ds(pl.multiple_of(j * LANES, LANES), LANES)
    taps = [window[k : k + 1, at] for k in range(TAPS)]
    for r in range(0, width, 16):
        rows = slice(r, r + 16)
        samples = [
            source[rows, pl.ds(pl.multiple_of(first + j * LANES, LANES), LANES)].astype(jnp.float32)
            for source, first in frames
        ]
        for f in range(STEP):
            total = samples[f] * taps[0]
            for k in range(1, TAPS):
                total = total + samples[f + k] * taps[k]
            filtered[f * width + r : f * width + r + 16, at] = total.astype(jnp.bfloat16)


def start_column(window, last, partial, j):
    at = pl.ds(pl.multiple_of(j * LANES, LANES), LANES)
    taps = [window[k : k + 1, at] for k in range(TAPS)]
    for r in range(0, last.shape[0], 16):
        rows = slice(r, r + 16)
        samples = [
            last[rows, pl.ds(pl.multiple_of(f * L + j * LANES, LANES), LANES)].astype(jnp.float32) for f in range(STEP)
        ]
        for f in range(STEP):
            total = samples[f] * taps[0]
            for k in range(1, STEP - f):
                total = total + samples[f + k] * taps[k]
            partial[f, rows, at] = total


def finish_column(window, partial, following, filtered, j):
    width = partial.shape[1]
    at = pl.ds(pl.multiple_of(j * LANES, LANES), LANES)
    taps = [window[k : k + 1, at] for k in range(TAPS)]
    for r in range(0, width, 16):
        rows = slice(r, r + 16)
        samples = [
            following[rows, pl.ds(pl.multiple_of(f * L + j * LANES, LANES), LANES)].astype(jnp.float32)
            for f in range(TAPS - 1)
        ]
        for f in range(STEP):
            total = partial[f, rows, at]
            for k in range(STEP - f, TAPS):
                total = total + samples[f + k - STEP] * taps[k]
            filtered[f * width + r : f * width + r + 16, at] = total.astype(jnp.bfloat16)


def filter_frames(window, frames, filtered, beside=None, start=0):
    def column(j, carry):
        filter_column(window, frames, filtered, j)
        return carry if beside is None else beside(j, carry)

    return lax.fori_loop(0, L // LANES, column, start)


def note_places(slots, places, channels, owner, empty):
    blocks = L // LANES
    per_owner = slots.shape[1] // blocks
    for k in range(per_owner):
        a, b = slots[0, owner * per_owner + k], slots[1, owner * per_owner + k]
        place = owner * (channels * per_owner) + k
        present = a >= 0
        places[jnp.where(present, a * blocks + b, blocks * blocks + empty)] = place
        empty = empty + jnp.where(present, 0, 1)
    return empty


def transform(table, filtered, spectra, columns, beside=None):
    rows = 512
    chunks = 2 * NCH // rows
    share = L // LANES // chunks

    def chunk(i, carry):
        at = pl.ds(pl.multiple_of(i * rows, rows), rows)
        product = lax.dot_general(
            table[at, :], filtered[...], (((1,), (1,)), ((), ())), preferred_element_type=jnp.float32
        )
        spectra[at, columns] = product.astype(jnp.bfloat16)
        if beside is not None:
            for j in range(share):
                beside(i * share + j)
        return carry

    lax.fori_loop(0, chunks, chunk, 0)


def early_kernel(
    channels, coarse_hbm, fine_hbm, window_hbm, slots_hbm, voltages, spectra, table, partial, window, places,
    coarse, fine, head, last, even, odd, slots, sems,
):
    span = STEP * L
    width = even.shape[0]
    steps = spectra.shape[1] // width
    small = [(coarse_hbm, coarse), (fine_hbm, fine), (window_hbm, window), (slots_hbm, slots)]
    loads = [pltpu.make_async_copy(source, target, sems.at[n]) for n, (source, target) in enumerate(small)]
    copies = []
    for n in range(steps):
        target = last if n == steps - 1 else head.at[:, n * span : (n + 1) * span]
        source = voltages.at[:, n * span : (n + 1) * span]
        copies.append(pltpu.make_async_copy(source, target, sems.at[len(small) + n]))
    for copy in loads + copies:
        copy.start()
    for copy in loads:
        copy.wait()
    build_table(coarse, fine, table)
    samples = [(head, f * L) for f in range((steps - 1) * STEP)] + [(last, f * L) for f in range(STEP)]
    frames = lambda n: samples[n * STEP : (n + 1) * STEP + TAPS - 1]
    copies[0].wait()
    copies[1].wait()
    filtered = [even, odd]
    note = lambda j, empty: note_places(slots, places, channels, j, empty)
    places[places.shape[0] - 1] = filter_frames(window, frames(0), even, note, 0)
    for n in range(steps - 1):
        beside = None
        if n < steps - 2:
            copies[n + 2].wait()
            beside = lambda j, n=n: filter_column(window, frames(n + 1), filtered[(n + 1) % 2], j)
        transform(table, filtered[n % 2], spectra, slice(n * width, (n + 1) * width), beside)

    def column(j, carry):
        start_column(window, last, partial, j)
        return carry

    lax.fori_loop(0, L // LANES, column, 0)


def late_kernel(table, window, partial, following, earlier, spectra, filtered):
    del earlier

    def column(j, carry):
        finish_column(window, partial, following, filtered, j)
        return carry

    lax.fori_loop(0, L // LANES, column, 0)
    first = spectra.shape[1] - filtered.shape[0]
    transform(table, filtered, spectra, slice(first, spectra.shape[1]))


def halo_kernel(voltages, halo, sem):
    copy = pltpu.make_async_copy(voltages.at[:, : halo.shape[1]], halo, sem)
    copy.start()
    copy.wait()


def in_hbm(array):
    return pltpu.with_memory_space_constraint(array, pltpu.HBM)


def channelize(voltages, tile_table, blocks, channels):
    width, local_len = voltages.shape
    steps = local_len // (STEP * L)
    span = STEP * L
    halo = (TAPS - 1) * L
    devices = lax.axis_size("chan")
    here = pl.BlockSpec(memory_space=pltpu.VMEM)
    hbm = pl.BlockSpec(memory_space=pltpu.HBM)
    first = pl.pallas_call(
        halo_kernel,
        name="halo",
        in_specs=[hbm],
        out_specs=here,
        out_shape=jax.ShapeDtypeStruct((width, halo), jnp.bfloat16),
        scratch_shapes=[pltpu.SemaphoreType.DMA],
        compiler_params=pltpu.CompilerParams(vmem_limit_bytes=2**20),
    )(in_hbm(voltages))
    following = lax.ppermute(first, "chan", [(i, i - 1) for i in range(1, devices)])
    constants = [*twiddle_factors(), filter_window()]
    assert blocks == L // LANES
    columns = STEP * width
    spectra_shape = jax.ShapeDtypeStruct((2 * NCH, steps * columns), jnp.bfloat16)
    filtered = pltpu.VMEM((columns, L), jnp.bfloat16)
    smem = pl.BlockSpec(memory_space=pltpu.SMEM)
    early, table, partial, window, places = pl.pallas_call(
        functools.partial(early_kernel, channels),
        name="channelize_early",
        in_specs=[hbm] * 5,
        out_specs=[here] * 4 + [smem],
        out_shape=[
            spectra_shape,
            jax.ShapeDtypeStruct((2 * NCH, L), jnp.bfloat16),
            jax.ShapeDtypeStruct((STEP, width, L), jnp.float32),
            jax.ShapeDtypeStruct((TAPS, L), jnp.float32),
            jax.ShapeDtypeStruct((blocks * blocks + tile_table.shape[0] + 1,), jnp.int32),
        ],
        scratch_shapes=[
            pltpu.VMEM(constants[0].shape, jnp.float32),
            pltpu.VMEM(constants[1].shape, jnp.float32),
            pltpu.VMEM((width, local_len - span), jnp.bfloat16),
            pltpu.VMEM((width, span), jnp.bfloat16),
            filtered,
            filtered,
            pltpu.SMEM(tile_table.shape[::-1], jnp.int32),
            pltpu.SemaphoreType.DMA((4 + steps,)),
        ],
        compiler_params=pltpu.CompilerParams(vmem_limit_bytes=24 * 2**20),
        cost_estimate=pl.CostEstimate(flops=3 * 10**9, bytes_accessed=12 * 2**20, transcendentals=0),
    )(*(in_hbm(jnp.asarray(t)) for t in constants), in_hbm(tile_table.T), in_hbm(voltages))
    spectra = pl.pallas_call(
        late_kernel,
        name="channelize_late",
        in_specs=[here] * 5,
        out_specs=here,
        out_shape=spectra_shape,
        scratch_shapes=[filtered],
        input_output_aliases={4: 0},
        compiler_params=pltpu.CompilerParams(vmem_limit_bytes=24 * 2**20),
        cost_estimate=pl.CostEstimate(flops=10**9, bytes_accessed=6 * 2**20, transcendentals=0),
    )(table, window, partial, following, early)
    return spectra, places


def gram_kernel(frame_total, places, spectra, tiles, wide, lefts, rights, row_scale, col_scale):
    channel = pl.program_id(0)
    width = tiles.shape[1]
    blocks = lefts.shape[0] // width
    owners = blocks
    channels = spectra.shape[1] // 2
    per_owner = tiles.shape[0] // (owners * channels)
    times = spectra.shape[0] // blocks
    pieces = spectra.shape[2] // LANES
    parts = spectra.shape[1]
    depth = times * pieces

    @pl.when(channel == 0)
    def _():
        def unpack(b, carry):
            for t in range(times):
                rows = spectra[t * blocks + b].astype(jnp.float32)
                for p in range(pieces):
                    at = (t * pieces + p) * parts
                    wide[b, at : at + parts, :] = rows[:, p * LANES : (p + 1) * LANES]
            return carry

        lax.fori_loop(0, blocks, unpack, 0)

        def clear(n, carry):
            for c in range(channels):
                tiles[places[blocks * blocks + n] + c * per_owner] = jnp.zeros((width, LANES), jnp.bfloat16)
            return carry

        lax.fori_loop(0, places[places.shape[0] - 1], clear, 0)

    low = lax.broadcasted_iota(jnp.int32, (depth, LANES), 1) < width
    turn = lambda x: pltpu.roll(x, LANES // 2, 1)

    def scale(power):
        return lax.rsqrt(power / frame_total + 1e-6)

    def build(q, carry):
        pair, factors = [], []
        for n in range(2):
            re = wide[2 * q + n, pl.ds(2 * channel, depth, stride=parts), :]
            im = wide[2 * q + n, pl.ds(2 * channel + 1, depth, stride=parts), :]
            power = jnp.sum(re * re + im * im, axis=0, keepdims=True)
            re, im = re.astype(jnp.bfloat16), im.astype(jnp.bfloat16)
            re_turned, im_turned = turn(re), turn(im)
            pair.append((re, re_turned, im, im_turned))
            lanes = slice(n * LANES, (n + 1) * LANES)
            right = (
                jnp.where(low, re, -im_turned),
                jnp.where(low, re_turned, -im),
                jnp.where(low, im, re_turned),
                jnp.where(low, im_turned, re),
            )
            for k, part in enumerate(right):
                rights[q, k * depth : (k + 1) * depth, lanes] = part
            factor = scale(power + turn(power))
            col_scale[q, :, lanes] = factor
            factors.append(factor)
        x, y = pair
        flat = [jnp.where(low, x[k], y[k ^ 1]) for k in range(4)]
        flat = jnp.concatenate(flat, axis=0).T
        rows = pl.ds(pl.multiple_of(q * LANES, LANES), LANES)
        lefts[rows, :] = flat
        factor = jnp.where(low[:1], factors[0], factors[1]) / frame_total
        row_scale[rows, :] = jnp.broadcast_to(factor, (8, LANES)).T[:, :1]
        return carry

    lax.fori_loop(0, blocks // 2, build, 0, unroll=2)

    offset = channel * per_owner
    for q in range(blocks // 2):
        for first in range(0, (q + 1) * LANES, 256):
            rows = slice(first, min(first + 256, (q + 1) * LANES))
            product = jnp.dot(lefts[rows, :], rights[q], preferred_element_type=jnp.float32)
            product = (product * row_scale[rows, :] * col_scale[q]).astype(jnp.bfloat16)
            for n in range(2):
                for a in range(rows.start // width, min(rows.stop // width, 2 * q + n + 1)):
                    start = a * width - rows.start
                    tile = product[start : start + width, n * LANES : (n + 1) * LANES]
                    tiles[places[a * blocks + 2 * q + n] + offset] = tile


def all_tiles(spectra, places, per_owner, blocks, width, frame_total):
    parts = spectra.shape[1]
    channels = parts // 2
    times = spectra.shape[0] // blocks
    depth = times * spectra.shape[2] // LANES
    return pl.pallas_call(
        functools.partial(gram_kernel, float(frame_total)),
        name="gram",
        grid_spec=pltpu.PrefetchScalarGridSpec(
            num_scalar_prefetch=1,
            grid=(channels,),
            in_specs=[pl.BlockSpec(spectra.shape, lambda c, s: (0, 0, 0), pipeline_mode=pl.Buffered(1))],
            out_specs=pl.BlockSpec(memory_space=pltpu.VMEM),
            scratch_shapes=[
                pltpu.VMEM((blocks, depth * parts, LANES), jnp.float32),
                pltpu.VMEM((blocks * width, 4 * depth), jnp.bfloat16),
                pltpu.VMEM((blocks // 2, 4 * depth, 2 * LANES), jnp.bfloat16),
                pltpu.VMEM((blocks * width, 1), jnp.float32),
                pltpu.VMEM((blocks // 2, 1, 2 * LANES), jnp.float32),
            ],
        ),
        out_shape=jax.ShapeDtypeStruct((blocks * channels * per_owner, width, 2 * width), jnp.bfloat16),
        compiler_params=pltpu.CompilerParams(vmem_limit_bytes=32 * 2**20),
        cost_estimate=pl.CostEstimate(flops=3 * 10**9, bytes_accessed=12 * 2**20, transcendentals=0),
    )(places, spectra)


def widen_kernel(tiles, out, held, sems):
    sources, channels = tiles.shape[:2]
    buffers = held.shape[0]
    copy = lambda d, n: pltpu.make_async_copy(held.at[n], out.at[d], sems.at[n])

    def source(d, carry):
        n = lax.rem(d, buffers)

        @pl.when(d >= buffers)
        def _():
            copy(d - buffers, n).wait()

        def channel(c, carry):
            held[n, c] = tiles[d, c].astype(jnp.float32)
            return carry

        lax.fori_loop(0, channels, channel, 0)
        copy(d, n).start()
        return carry

    lax.fori_loop(0, sources, source, 0)
    for d in range(sources - buffers, sources):
        copy(d, d % buffers).wait()


def widen(tiles):
    buffers = 8
    return pl.pallas_call(
        widen_kernel,
        name="widen",
        in_specs=[pl.BlockSpec(memory_space=pltpu.VMEM)],
        out_specs=pl.BlockSpec(memory_space=pltpu.HBM),
        out_shape=jax.ShapeDtypeStruct(tiles.shape, jnp.float32),
        scratch_shapes=[pltpu.VMEM((buffers, *tiles.shape[1:]), jnp.float32), pltpu.SemaphoreType.DMA((buffers,))],
        compiler_params=pltpu.CompilerParams(vmem_limit_bytes=24 * 2**20),
        cost_estimate=pl.CostEstimate(flops=0, bytes_accessed=28 * 2**20, transcendentals=0),
    )(tiles)


def on_device(voltages, tile_table):
    width, local_len = voltages.shape
    blocks = lax.axis_size("inp")
    devices = blocks * lax.axis_size("chan")
    frame_total = local_len // L * lax.axis_size("chan")
    channels = NCH // devices
    per_owner = tile_table.shape[0] // blocks
    spectra, places = channelize(voltages, tile_table, blocks, channels)
    spectra = spectra.reshape(devices, 2 * channels, spectra.shape[1])
    turned = lax.all_to_all(spectra, EVERY, 0, 0, tiled=True)
    tiles = all_tiles(turned, places, per_owner, blocks, width, frame_total)
    tiles = tiles.reshape(blocks, channels, per_owner, *tiles.shape[1:])
    out = widen(lax.all_to_all(tiles, "inp", 0, 0, tiled=True))
    return out.reshape(-1, *out.shape[2:])


def solution(mesh):
    return jax.shard_map(
        on_device,
        mesh=mesh,
        in_specs=(P("inp", "chan"), P()),
        out_specs=P("chan", "inp", None, None),
        check_vma=False,
    )
```

```python
import functools
import math

import jax
import jax.numpy as jnp
import numpy as np
from jax import lax
from jax.experimental import pallas as pl
from jax.experimental.pallas import tpu as pltpu
from jax.sharding import PartitionSpec as P

L = 2048
NCH = 512
TAPS = 4
LANES = 128
STEP = 4
COARSE = 16
EVERY = ("chan", "inp")


def filter_window():
    positions = np.arange(TAPS * L, dtype=np.float64)
    tapering = 0.5 - 0.5 * np.cos(2.0 * math.pi * positions / (TAPS * L))
    shape_sinc = np.sinc((positions - TAPS * L / 2.0) / L)
    return (shape_sinc * tapering).reshape(TAPS, L).astype(np.float32)


def twiddle_factors():
    unit = 2.0 * math.pi / L
    coarse = (COARSE * np.arange(NCH // COARSE)[:, None] * np.arange(L // COARSE)[None, :]) % L
    rows = np.arange(2 * COARSE)[:, None]
    fine = ((rows // 2) * np.arange(L // 2)[None, :] + (rows % 2) * (L // 4)) % L
    both = lambda phases: np.concatenate([np.cos(phases * unit), np.sin(phases * unit)]).astype(np.float32)
    return both(coarse), both(fine)


def build_table(coarse, fine, table):
    rows = 2 * COARSE
    groups = NCH // COARSE
    channel = lax.broadcasted_iota(jnp.int32, (rows, LANES), 0) // 2
    later = jnp.where(channel % 2 == 0, 1.0, -1.0).astype(jnp.float32)

    def column(j, carry):
        lanes = pl.ds(pl.multiple_of(j * LANES, LANES), LANES)
        lanes_later = pl.ds(pl.multiple_of(j * LANES + L // 2, LANES), LANES)
        fine_cos, fine_sin = fine[:rows, lanes], fine[rows:, lanes]
        for a in range(groups):
            part = coarse[a : a + 1, :] * fine_cos - coarse[groups + a : groups + a + 1, :] * fine_sin
            table[a * rows : (a + 1) * rows, lanes] = part.astype(jnp.bfloat16)
            table[a * rows : (a + 1) * rows, lanes_later] = (part * later).astype(jnp.bfloat16)
        return carry

    lax.fori_loop(0, L // 2 // LANES, column, 0)


def filter_column(window, frames, filtered, j):
    width = frames[0][0].shape[0]
    at = pl.ds(pl.multiple_of(j * LANES, LANES), LANES)
    taps = [window[k : k + 1, at] for k in range(TAPS)]
    for r in range(0, width, 16):
        rows = slice(r, r + 16)
        samples = [
            source[rows, pl.ds(pl.multiple_of(first + j * LANES, LANES), LANES)].astype(jnp.float32)
            for source, first in frames
        ]
        for f in range(STEP):
            total = samples[f] * taps[0]
            for k in range(1, TAPS):
                total = total + samples[f + k] * taps[k]
            filtered[f * width + r : f * width + r + 16, at] = total.astype(jnp.bfloat16)


def start_column(window, last, partial, j):
    at = pl.ds(pl.multiple_of(j * LANES, LANES), LANES)
    taps = [window[k : k + 1, at] for k in range(TAPS)]
    for r in range(0, last.shape[0], 16):
        rows = slice(r, r + 16)
        samples = [
            last[rows, pl.ds(pl.multiple_of(f * L + j * LANES, LANES), LANES)].astype(jnp.float32) for f in range(STEP)
        ]
        for f in range(STEP):
            total = samples[f] * taps[0]
            for k in range(1, STEP - f):
                total = total + samples[f + k] * taps[k]
            partial[f, rows, at] = total


def finish_column(window, partial, following, filtered, j):
    width = partial.shape[1]
    at = pl.ds(pl.multiple_of(j * LANES, LANES), LANES)
    taps = [window[k : k + 1, at] for k in range(TAPS)]
    for r in range(0, width, 16):
        rows = slice(r, r + 16)
        samples = [
            following[rows, pl.ds(pl.multiple_of(f * L + j * LANES, LANES), LANES)].astype(jnp.float32)
            for f in range(TAPS - 1)
        ]
        for f in range(STEP):
            total = partial[f, rows, at]
            for k in range(STEP - f, TAPS):
                total = total + samples[f + k - STEP] * taps[k]
            filtered[f * width + r : f * width + r + 16, at] = total.astype(jnp.bfloat16)


def filter_frames(window, frames, filtered, beside=None, start=0):
    def column(j, carry):
        filter_column(window, frames, filtered, j)
        return carry if beside is None else beside(j, carry)

    return lax.fori_loop(0, L // LANES, column, start)


def note_places(slots, places, channels, owner, empty):
    blocks = L // LANES
    per_owner = slots.shape[1] // blocks
    for k in range(per_owner):
        a, b = slots[0, owner * per_owner + k], slots[1, owner * per_owner + k]
        place = owner * (channels * per_owner) + k
        present = a >= 0
        places[jnp.where(present, a * blocks + b, blocks * blocks + empty)] = place
        empty = empty + jnp.where(present, 0, 1)
    return empty


def transform(table, filtered, spectra, columns, beside=None):
    rows = 512
    chunks = 2 * NCH // rows
    share = L // LANES // chunks

    def chunk(i, carry):
        at = pl.ds(pl.multiple_of(i * rows, rows), rows)
        product = lax.dot_general(
            table[at, :], filtered[...], (((1,), (1,)), ((), ())), preferred_element_type=jnp.float32
        )
        spectra[at, columns] = product.astype(jnp.bfloat16)
        if beside is not None:
            for j in range(share):
                beside(i * share + j)
        return carry

    lax.fori_loop(0, chunks, chunk, 0)


def early_kernel(
    channels, coarse_hbm, fine_hbm, window_hbm, slots_hbm, voltages, spectra, table, partial, window, places,
    coarse, fine, head, last, even, odd, slots, sems,
):
    span = STEP * L
    width = even.shape[0]
    steps = spectra.shape[1] // width
    small = [(coarse_hbm, coarse), (fine_hbm, fine), (window_hbm, window), (slots_hbm, slots)]
    loads = [pltpu.make_async_copy(source, target, sems.at[n]) for n, (source, target) in enumerate(small)]
    copies = []
    for n in range(steps):
        target = last if n == steps - 1 else head.at[:, n * span : (n + 1) * span]
        source = voltages.at[:, n * span : (n + 1) * span]
        copies.append(pltpu.make_async_copy(source, target, sems.at[len(small) + n]))
    for copy in loads + copies:
        copy.start()
    for copy in loads:
        copy.wait()
    build_table(coarse, fine, table)
    samples = [(head, f * L) for f in range((steps - 1) * STEP)] + [(last, f * L) for f in range(STEP)]
    frames = lambda n: samples[n * STEP : (n + 1) * STEP + TAPS - 1]
    copies[0].wait()
    copies[1].wait()
    filtered = [even, odd]
    note = lambda j, empty: note_places(slots, places, channels, j, empty)
    places[places.shape[0] - 1] = filter_frames(window, frames(0), even, note, 0)
    for n in range(steps - 1):
        beside = None
        if n < steps - 2:
            copies[n + 2].wait()
            beside = lambda j, n=n: filter_column(window, frames(n + 1), filtered[(n + 1) % 2], j)
        transform(table, filtered[n % 2], spectra, slice(n * width, (n + 1) * width), beside)

    def column(j, carry):
        start_column(window, last, partial, j)
        return carry

    lax.fori_loop(0, L // LANES, column, 0)


def late_kernel(table, window, partial, following, earlier, spectra, filtered):
    del earlier

    def column(j, carry):
        finish_column(window, partial, following, filtered, j)
        return carry

    lax.fori_loop(0, L // LANES, column, 0)
    first = spectra.shape[1] - filtered.shape[0]
    transform(table, filtered, spectra, slice(first, spectra.shape[1]))


def halo_kernel(voltages, halo, sem):
    copy = pltpu.make_async_copy(voltages.at[:, : halo.shape[1]], halo, sem)
    copy.start()
    copy.wait()


def in_hbm(array):
    return pltpu.with_memory_space_constraint(array, pltpu.HBM)


def channelize(voltages, tile_table, blocks, channels):
    width, local_len = voltages.shape
    steps = local_len // (STEP * L)
    span = STEP * L
    halo = (TAPS - 1) * L
    devices = lax.axis_size("chan")
    here = pl.BlockSpec(memory_space=pltpu.VMEM)
    hbm = pl.BlockSpec(memory_space=pltpu.HBM)
    first = pl.pallas_call(
        halo_kernel,
        name="halo",
        in_specs=[hbm],
        out_specs=here,
        out_shape=jax.ShapeDtypeStruct((width, halo), jnp.bfloat16),
        scratch_shapes=[pltpu.SemaphoreType.DMA],
        compiler_params=pltpu.CompilerParams(vmem_limit_bytes=2**20),
    )(in_hbm(voltages))
    following = lax.ppermute(first, "chan", [(i, i - 1) for i in range(1, devices)])
    constants = [*twiddle_factors(), filter_window()]
    assert blocks == L // LANES
    columns = STEP * width
    spectra_shape = jax.ShapeDtypeStruct((2 * NCH, steps * columns), jnp.bfloat16)
    filtered = pltpu.VMEM((columns, L), jnp.bfloat16)
    smem = pl.BlockSpec(memory_space=pltpu.SMEM)
    early, table, partial, window, places = pl.pallas_call(
        functools.partial(early_kernel, channels),
        name="channelize_early",
        in_specs=[hbm] * 5,
        out_specs=[here] * 4 + [smem],
        out_shape=[
            spectra_shape,
            jax.ShapeDtypeStruct((2 * NCH, L), jnp.bfloat16),
            jax.ShapeDtypeStruct((STEP, width, L), jnp.float32),
            jax.ShapeDtypeStruct((TAPS, L), jnp.float32),
            jax.ShapeDtypeStruct((blocks * blocks + tile_table.shape[0] + 1,), jnp.int32),
        ],
        scratch_shapes=[
            pltpu.VMEM(constants[0].shape, jnp.float32),
            pltpu.VMEM(constants[1].shape, jnp.float32),
            pltpu.VMEM((width, local_len - span), jnp.bfloat16),
            pltpu.VMEM((width, span), jnp.bfloat16),
            filtered,
            filtered,
            pltpu.SMEM(tile_table.shape[::-1], jnp.int32),
            pltpu.SemaphoreType.DMA((4 + steps,)),
        ],
        compiler_params=pltpu.CompilerParams(vmem_limit_bytes=24 * 2**20),
        cost_estimate=pl.CostEstimate(flops=3 * 10**9, bytes_accessed=12 * 2**20, transcendentals=0),
    )(*(in_hbm(jnp.asarray(t)) for t in constants), in_hbm(tile_table.T), in_hbm(voltages))
    spectra = pl.pallas_call(
        late_kernel,
        name="channelize_late",
        in_specs=[here] * 5,
        out_specs=here,
        out_shape=spectra_shape,
        scratch_shapes=[filtered],
        input_output_aliases={4: 0},
        compiler_params=pltpu.CompilerParams(vmem_limit_bytes=24 * 2**20),
        cost_estimate=pl.CostEstimate(flops=10**9, bytes_accessed=6 * 2**20, transcendentals=0),
    )(table, window, partial, following, early)
    return spectra, places


def gram_kernel(frame_total, places, spectra, tiles, wide, lefts, rights, row_scale, col_scale):
    channel = pl.program_id(0)
    width = tiles.shape[1]
    blocks = lefts.shape[0] // width
    owners = blocks
    channels = spectra.shape[1] // 2
    per_owner = tiles.shape[0] // (owners * channels)
    times = spectra.shape[0] // blocks
    pieces = spectra.shape[2] // LANES
    parts = spectra.shape[1]
    depth = times * pieces

    @pl.when(channel == 0)
    def _():
        def unpack(b, carry):
            for t in range(times):
                rows = spectra[t * blocks + b].astype(jnp.float32)
                for p in range(pieces):
                    at = (t * pieces + p) * parts
                    wide[b, at : at + parts, :] = rows[:, p * LANES : (p + 1) * LANES]
            return carry

        lax.fori_loop(0, blocks, unpack, 0)

        def clear(n, carry):
            for c in range(channels):
                tiles[places[blocks * blocks + n] + c * per_owner] = jnp.zeros((width, LANES), jnp.bfloat16)
            return carry

        lax.fori_loop(0, places[places.shape[0] - 1], clear, 0)

    low = lax.broadcasted_iota(jnp.int32, (depth, LANES), 1) < width
    turn = lambda x: pltpu.roll(x, LANES // 2, 1)

    def scale(power):
        return lax.rsqrt(power / frame_total + 1e-6)

    def build(q, carry):
        pair, factors = [], []
        for n in range(2):
            re = wide[2 * q + n, pl.ds(2 * channel, depth, stride=parts), :]
            im = wide[2 * q + n, pl.ds(2 * channel + 1, depth, stride=parts), :]
            power = jnp.sum(re * re + im * im, axis=0, keepdims=True)
            re, im = re.astype(jnp.bfloat16), im.astype(jnp.bfloat16)
            re_turned, im_turned = turn(re), turn(im)
            pair.append((re, re_turned, im, im_turned))
            lanes = slice(n * LANES, (n + 1) * LANES)
            right = (
                jnp.where(low, re, -im_turned),
                jnp.where(low, re_turned, -im),
                jnp.where(low, im, re_turned),
                jnp.where(low, im_turned, re),
            )
            for k, part in enumerate(right):
                rights[q, k * depth : (k + 1) * depth, lanes] = part
            factor = scale(power + turn(power))
            col_scale[q, :, lanes] = factor
            factors.append(factor)
        x, y = pair
        flat = [jnp.where(low, x[k], y[k ^ 1]) for k in range(4)]
        flat = jnp.concatenate(flat, axis=0).T
        rows = pl.ds(pl.multiple_of(q * LANES, LANES), LANES)
        lefts[rows, :] = flat
        factor = jnp.where(low[:1], factors[0], factors[1]) / frame_total
        row_scale[rows, :] = jnp.broadcast_to(factor, (LANES, LANES)).T
        return carry

    lax.fori_loop(0, blocks // 2, build, 0, unroll=2)

    offset = channel * per_owner
    for q in range(blocks // 2):
        for first in range(0, (q + 1) * LANES, 256):
            rows = slice(first, min(first + 256, (q + 1) * LANES))
            product = jnp.dot(lefts[rows, :], rights[q], preferred_element_type=jnp.float32)
            for n in range(2):
                lanes = slice(n * LANES, (n + 1) * LANES)
                part = (product[:, lanes] * row_scale[rows, :] * col_scale[q, :, lanes]).astype(jnp.bfloat16)
                for a in range(rows.start // width, min(rows.stop // width, 2 * q + n + 1)):
                    start = a * width - rows.start
                    tiles[places[a * blocks + 2 * q + n] + offset] = part[start : start + width, :]


def all_tiles(spectra, places, per_owner, blocks, width, frame_total):
    parts = spectra.shape[1]
    channels = parts // 2
    times = spectra.shape[0] // blocks
    depth = times * spectra.shape[2] // LANES
    return pl.pallas_call(
        functools.partial(gram_kernel, float(frame_total)),
        name="gram",
        grid_spec=pltpu.PrefetchScalarGridSpec(
            num_scalar_prefetch=1,
            grid=(channels,),
            in_specs=[pl.BlockSpec(spectra.shape, lambda c, s: (0, 0, 0), pipeline_mode=pl.Buffered(1))],
            out_specs=pl.BlockSpec(memory_space=pltpu.VMEM),
            scratch_shapes=[
                pltpu.VMEM((blocks, depth * parts, LANES), jnp.float32),
                pltpu.VMEM((blocks * width, 4 * depth), jnp.bfloat16),
                pltpu.VMEM((blocks // 2, 4 * depth, 2 * LANES), jnp.bfloat16),
                pltpu.VMEM((blocks * width, LANES), jnp.float32),
                pltpu.VMEM((blocks // 2, 1, 2 * LANES), jnp.float32),
            ],
        ),
        out_shape=jax.ShapeDtypeStruct((blocks * channels * per_owner, width, 2 * width), jnp.bfloat16),
        compiler_params=pltpu.CompilerParams(vmem_limit_bytes=32 * 2**20),
        cost_estimate=pl.CostEstimate(flops=3 * 10**9, bytes_accessed=12 * 2**20, transcendentals=0),
    )(places, spectra)


def widen_kernel(tiles, out, held, sems):
    sources, channels = tiles.shape[:2]
    buffers = held.shape[0]
    copy = lambda d, n: pltpu.make_async_copy(held.at[n], out.at[d], sems.at[n])

    def source(d, carry):
        n = lax.rem(d, buffers)

        @pl.when(d >= buffers)
        def _():
            copy(d - buffers, n).wait()

        def channel(c, carry):
            held[n, c] = tiles[d, c].astype(jnp.float32)
            return carry

        lax.fori_loop(0, channels, channel, 0)
        copy(d, n).start()
        return carry

    lax.fori_loop(0, sources, source, 0)
    for d in range(sources - buffers, sources):
        copy(d, d % buffers).wait()


def widen(tiles):
    buffers = 8
    return pl.pallas_call(
        widen_kernel,
        name="widen",
        in_specs=[pl.BlockSpec(memory_space=pltpu.VMEM)],
        out_specs=pl.BlockSpec(memory_space=pltpu.HBM),
        out_shape=jax.ShapeDtypeStruct(tiles.shape, jnp.float32),
        scratch_shapes=[pltpu.VMEM((buffers, *tiles.shape[1:]), jnp.float32), pltpu.SemaphoreType.DMA((buffers,))],
        compiler_params=pltpu.CompilerParams(vmem_limit_bytes=24 * 2**20),
        cost_estimate=pl.CostEstimate(flops=0, bytes_accessed=28 * 2**20, transcendentals=0),
    )(tiles)


def on_device(voltages, tile_table):
    width, local_len = voltages.shape
    blocks = lax.axis_size("inp")
    devices = blocks * lax.axis_size("chan")
    frame_total = local_len // L * lax.axis_size("chan")
    channels = NCH // devices
    per_owner = tile_table.shape[0] // blocks
    spectra, places = channelize(voltages, tile_table, blocks, channels)
    spectra = spectra.reshape(devices, 2 * channels, spectra.shape[1])
    turned = lax.all_to_all(spectra, EVERY, 0, 0, tiled=True)
    tiles = all_tiles(turned, places, per_owner, blocks, width, frame_total)
    tiles = tiles.reshape(blocks, channels, per_owner, *tiles.shape[1:])
    out = widen(lax.all_to_all(tiles, "inp", 0, 0, tiled=True))
    return out.reshape(-1, *out.shape[2:])


def solution(mesh):
    return jax.shard_map(
        on_device,
        mesh=mesh,
        in_specs=(P("inp", "chan"), P()),
        out_specs=P("chan", "inp", None, None),
        check_vma=False,
    )
```

```python
import functools
import math

import jax
import jax.numpy as jnp
import numpy as np
from jax import lax
from jax.experimental import pallas as pl
from jax.experimental.pallas import tpu as pltpu
from jax.sharding import PartitionSpec as P

L = 2048
NCH = 512
TAPS = 4
LANES = 128
STEP = 4
COARSE = 16
EVERY = ("chan", "inp")


def filter_window():
    positions = np.arange(TAPS * L, dtype=np.float64)
    tapering = 0.5 - 0.5 * np.cos(2.0 * math.pi * positions / (TAPS * L))
    shape_sinc = np.sinc((positions - TAPS * L / 2.0) / L)
    return (shape_sinc * tapering).reshape(TAPS, L).astype(np.float32)


def twiddle_factors():
    unit = 2.0 * math.pi / L
    coarse = (COARSE * np.arange(NCH // COARSE)[:, None] * np.arange(L // COARSE)[None, :]) % L
    rows = np.arange(2 * COARSE)[:, None]
    fine = ((rows // 2) * np.arange(L // 2)[None, :] + (rows % 2) * (L // 4)) % L
    both = lambda phases: np.concatenate([np.cos(phases * unit), np.sin(phases * unit)]).astype(np.float32)
    return both(coarse), both(fine)


def build_table(coarse, fine, table):
    rows = 2 * COARSE
    groups = NCH // COARSE
    channel = lax.broadcasted_iota(jnp.int32, (rows, LANES), 0) // 2
    later = jnp.where(channel % 2 == 0, 1.0, -1.0).astype(jnp.float32)

    def column(j, carry):
        lanes = pl.ds(pl.multiple_of(j * LANES, LANES), LANES)
        lanes_later = pl.ds(pl.multiple_of(j * LANES + L // 2, LANES), LANES)
        fine_cos, fine_sin = fine[:rows, lanes], fine[rows:, lanes]
        for a in range(groups):
            part = coarse[a : a + 1, :] * fine_cos - coarse[groups + a : groups + a + 1, :] * fine_sin
            table[a * rows : (a + 1) * rows, lanes] = part.astype(jnp.bfloat16)
            table[a * rows : (a + 1) * rows, lanes_later] = (part * later).astype(jnp.bfloat16)
        return carry

    lax.fori_loop(0, L // 2 // LANES, column, 0)


def filter_column(window, frames, filtered, j):
    width = frames[0][0].shape[0]
    at = pl.ds(pl.multiple_of(j * LANES, LANES), LANES)
    taps = [window[k : k + 1, at] for k in range(TAPS)]
    for r in range(0, width, 16):
        rows = slice(r, r + 16)
        samples = [
            source[rows, pl.ds(pl.multiple_of(first + j * LANES, LANES), LANES)].astype(jnp.float32)
            for source, first in frames
        ]
        for f in range(STEP):
            total = samples[f] * taps[0]
            for k in range(1, TAPS):
                total = total + samples[f + k] * taps[k]
            filtered[f * width + r : f * width + r + 16, at] = total.astype(jnp.bfloat16)


def start_column(window, last, partial, j):
    at = pl.ds(pl.multiple_of(j * LANES, LANES), LANES)
    taps = [window[k : k + 1, at] for k in range(TAPS)]
    for r in range(0, last.shape[0], 16):
        rows = slice(r, r + 16)
        samples = [
            last[rows, pl.ds(pl.multiple_of(f * L + j * LANES, LANES), LANES)].astype(jnp.float32) for f in range(STEP)
        ]
        for f in range(STEP):
            total = samples[f] * taps[0]
            for k in range(1, STEP - f):
                total = total + samples[f + k] * taps[k]
            partial[f, rows, at] = total


def finish_column(window, partial, following, filtered, j):
    width = partial.shape[1]
    at = pl.ds(pl.multiple_of(j * LANES, LANES), LANES)
    taps = [window[k : k + 1, at] for k in range(TAPS)]
    for r in range(0, width, 16):
        rows = slice(r, r + 16)
        samples = [
            following[rows, pl.ds(pl.multiple_of(f * L + j * LANES, LANES), LANES)].astype(jnp.float32)
            for f in range(TAPS - 1)
        ]
        for f in range(STEP):
            total = partial[f, rows, at]
            for k in range(STEP - f, TAPS):
                total = total + samples[f + k - STEP] * taps[k]
            filtered[f * width + r : f * width + r + 16, at] = total.astype(jnp.bfloat16)


def filter_frames(window, frames, filtered, beside=None, start=0):
    def column(j, carry):
        filter_column(window, frames, filtered, j)
        return carry if beside is None else beside(j, carry)

    return lax.fori_loop(0, L // LANES, column, start)


def note_places(slots, places, channels, owner, empty):
    blocks = L // LANES
    per_owner = slots.shape[1] // blocks
    for k in range(per_owner):
        a, b = slots[0, owner * per_owner + k], slots[1, owner * per_owner + k]
        place = owner * (channels * per_owner) + k
        present = a >= 0
        places[jnp.where(present, a * blocks + b, blocks * blocks + empty)] = place
        empty = empty + jnp.where(present, 0, 1)
    return empty


def transform(table, filtered, spectra, columns, beside=None, rows=512):
    chunks = 2 * NCH // rows
    share = L // LANES // chunks

    def chunk(i, carry):
        at = pl.ds(pl.multiple_of(i * rows, rows), rows)
        product = lax.dot_general(
            table[at, :], filtered[...], (((1,), (1,)), ((), ())), preferred_element_type=jnp.float32
        )
        spectra[at, columns] = product.astype(jnp.bfloat16)
        if beside is not None:
            for j in range(share):
                beside(i * share + j)
        return carry

    lax.fori_loop(0, chunks, chunk, 0)


def early_kernel(
    channels, coarse_hbm, fine_hbm, window_hbm, slots_hbm, voltages, spectra, table, partial, window, places,
    coarse, fine, head, last, even, odd, slots, sems,
):
    span = STEP * L
    width = even.shape[0]
    steps = spectra.shape[1] // width
    small = [(coarse_hbm, coarse), (fine_hbm, fine), (window_hbm, window), (slots_hbm, slots)]
    loads = [pltpu.make_async_copy(source, target, sems.at[n]) for n, (source, target) in enumerate(small)]
    copies = []
    for n in range(steps):
        target = last if n == steps - 1 else head.at[:, n * span : (n + 1) * span]
        source = voltages.at[:, n * span : (n + 1) * span]
        copies.append(pltpu.make_async_copy(source, target, sems.at[len(small) + n]))
    for copy in loads + copies:
        copy.start()
    for copy in loads:
        copy.wait()
    build_table(coarse, fine, table)
    samples = [(head, f * L) for f in range((steps - 1) * STEP)] + [(last, f * L) for f in range(STEP)]
    frames = lambda n: samples[n * STEP : (n + 1) * STEP + TAPS - 1]
    copies[0].wait()
    copies[1].wait()
    filtered = [even, odd]
    note = lambda j, empty: note_places(slots, places, channels, j, empty)
    places[places.shape[0] - 1] = filter_frames(window, frames(0), even, note, 0)
    for n in range(steps - 1):
        beside = None
        if n < steps - 2:
            copies[n + 2].wait()
            beside = lambda j, n=n: filter_column(window, frames(n + 1), filtered[(n + 1) % 2], j)
        transform(table, filtered[n % 2], spectra, slice(n * width, (n + 1) * width), beside)

    def column(j, carry):
        start_column(window, last, partial, j)
        return carry

    lax.fori_loop(0, L // LANES, column, 0)


def late_kernel(table, window, partial, following, earlier, spectra, filtered):
    del earlier

    def column(j, carry):
        finish_column(window, partial, following, filtered, j)
        return carry

    lax.fori_loop(0, L // LANES, column, 0)
    first = spectra.shape[1] - filtered.shape[0]
    transform(table, filtered, spectra, slice(first, spectra.shape[1]), rows=2 * NCH)


def halo_kernel(voltages, halo, sem):
    copy = pltpu.make_async_copy(voltages.at[:, : halo.shape[1]], halo, sem)
    copy.start()
    copy.wait()


def in_hbm(array):
    return pltpu.with_memory_space_constraint(array, pltpu.HBM)


def channelize(voltages, tile_table, blocks, channels):
    width, local_len = voltages.shape
    steps = local_len // (STEP * L)
    span = STEP * L
    halo = (TAPS - 1) * L
    devices = lax.axis_size("chan")
    here = pl.BlockSpec(memory_space=pltpu.VMEM)
    hbm = pl.BlockSpec(memory_space=pltpu.HBM)
    first = pl.pallas_call(
        halo_kernel,
        name="halo",
        in_specs=[hbm],
        out_specs=here,
        out_shape=jax.ShapeDtypeStruct((width, halo), jnp.bfloat16),
        scratch_shapes=[pltpu.SemaphoreType.DMA],
        compiler_params=pltpu.CompilerParams(vmem_limit_bytes=2**20),
    )(in_hbm(voltages))
    following = lax.ppermute(first, "chan", [(i, i - 1) for i in range(1, devices)])
    constants = [*twiddle_factors(), filter_window()]
    assert blocks == L // LANES
    columns = STEP * width
    spectra_shape = jax.ShapeDtypeStruct((2 * NCH, steps * columns), jnp.bfloat16)
    filtered = pltpu.VMEM((columns, L), jnp.bfloat16)
    smem = pl.BlockSpec(memory_space=pltpu.SMEM)
    early, table, partial, window, places = pl.pallas_call(
        functools.partial(early_kernel, channels),
        name="channelize_early",
        in_specs=[hbm] * 5,
        out_specs=[here] * 4 + [smem],
        out_shape=[
            spectra_shape,
            jax.ShapeDtypeStruct((2 * NCH, L), jnp.bfloat16),
            jax.ShapeDtypeStruct((STEP, width, L), jnp.float32),
            jax.ShapeDtypeStruct((TAPS, L), jnp.float32),
            jax.ShapeDtypeStruct((blocks * blocks + tile_table.shape[0] + 1,), jnp.int32),
        ],
        scratch_shapes=[
            pltpu.VMEM(constants[0].shape, jnp.float32),
            pltpu.VMEM(constants[1].shape, jnp.float32),
            pltpu.VMEM((width, local_len - span), jnp.bfloat16),
            pltpu.VMEM((width, span), jnp.bfloat16),
            filtered,
            filtered,
            pltpu.SMEM(tile_table.shape[::-1], jnp.int32),
            pltpu.SemaphoreType.DMA((4 + steps,)),
        ],
        compiler_params=pltpu.CompilerParams(vmem_limit_bytes=24 * 2**20),
        cost_estimate=pl.CostEstimate(flops=3 * 10**9, bytes_accessed=12 * 2**20, transcendentals=0),
    )(*(in_hbm(jnp.asarray(t)) for t in constants), in_hbm(tile_table.T), in_hbm(voltages))
    spectra = pl.pallas_call(
        late_kernel,
        name="channelize_late",
        in_specs=[here] * 5,
        out_specs=here,
        out_shape=spectra_shape,
        scratch_shapes=[filtered],
        input_output_aliases={4: 0},
        compiler_params=pltpu.CompilerParams(vmem_limit_bytes=24 * 2**20),
        cost_estimate=pl.CostEstimate(flops=10**9, bytes_accessed=6 * 2**20, transcendentals=0),
    )(table, window, partial, following, early)
    return spectra, places


def gram_kernel(frame_total, places, spectra, tiles, wide, lefts, rights, row_scale, col_scale):
    channel = pl.program_id(0)
    width = tiles.shape[1]
    blocks = lefts.shape[0] // width
    owners = blocks
    channels = spectra.shape[1] // 2
    per_owner = tiles.shape[0] // (owners * channels)
    times = spectra.shape[0] // blocks
    pieces = spectra.shape[2] // LANES
    parts = spectra.shape[1]
    depth = times * pieces

    @pl.when(channel == 0)
    def _():
        def unpack(b, carry):
            for t in range(times):
                rows = spectra[t * blocks + b].astype(jnp.float32)
                for p in range(pieces):
                    at = (t * pieces + p) * parts
                    wide[b, at : at + parts, :] = rows[:, p * LANES : (p + 1) * LANES]
            return carry

        lax.fori_loop(0, blocks, unpack, 0)

        def clear(n, carry):
            for c in range(channels):
                tiles[places[blocks * blocks + n] + c * per_owner] = jnp.zeros((width, LANES), jnp.bfloat16)
            return carry

        lax.fori_loop(0, places[places.shape[0] - 1], clear, 0)

    low = lax.broadcasted_iota(jnp.int32, (depth, LANES), 1) < width
    turn = lambda x: pltpu.roll(x, LANES // 2, 1)

    def scale(power):
        return lax.rsqrt(power / frame_total + 1e-6)

    def build(q, carry):
        pair, factors = [], []
        for n in range(2):
            re = wide[2 * q + n, pl.ds(2 * channel, depth, stride=parts), :]
            im = wide[2 * q + n, pl.ds(2 * channel + 1, depth, stride=parts), :]
            power = jnp.sum(re * re + im * im, axis=0, keepdims=True)
            re, im = re.astype(jnp.bfloat16), im.astype(jnp.bfloat16)
            re_turned, im_turned = turn(re), turn(im)
            pair.append((re, re_turned, im, im_turned))
            lanes = slice(n * LANES, (n + 1) * LANES)
            right = (
                jnp.where(low, re, -im_turned),
                jnp.where(low, re_turned, -im),
                jnp.where(low, im, re_turned),
                jnp.where(low, im_turned, re),
            )
            for k, part in enumerate(right):
                rights[q, k * depth : (k + 1) * depth, lanes] = part
            factor = scale(power + turn(power))
            col_scale[q, :, lanes] = factor
            factors.append(factor)
        x, y = pair
        flat = [jnp.where(low, x[k], y[k ^ 1]) for k in range(4)]
        flat = jnp.concatenate(flat, axis=0).T
        rows = pl.ds(pl.multiple_of(q * LANES, LANES), LANES)
        lefts[rows, :] = flat
        factor = jnp.where(low[:1], factors[0], factors[1]) / frame_total
        row_scale[rows, :] = jnp.broadcast_to(factor, (LANES, LANES)).T
        return carry

    lax.fori_loop(0, blocks // 2, build, 0, unroll=2)

    offset = channel * per_owner
    for q in range(blocks // 2):
        for first in range(0, (q + 1) * LANES, 256):
            rows = slice(first, min(first + 256, (q + 1) * LANES))
            product = jnp.dot(lefts[rows, :], rights[q], preferred_element_type=jnp.float32)
            for n in range(2):
                lanes = slice(n * LANES, (n + 1) * LANES)
                part = (product[:, lanes] * row_scale[rows, :] * col_scale[q, :, lanes]).astype(jnp.bfloat16)
                for a in range(rows.start // width, min(rows.stop // width, 2 * q + n + 1)):
                    start = a * width - rows.start
                    tiles[places[a * blocks + 2 * q + n] + offset] = part[start : start + width, :]


def all_tiles(spectra, places, per_owner, blocks, width, frame_total):
    parts = spectra.shape[1]
    channels = parts // 2
    times = spectra.shape[0] // blocks
    depth = times * spectra.shape[2] // LANES
    return pl.pallas_call(
        functools.partial(gram_kernel, float(frame_total)),
        name="gram",
        grid_spec=pltpu.PrefetchScalarGridSpec(
            num_scalar_prefetch=1,
            grid=(channels,),
            in_specs=[pl.BlockSpec(spectra.shape, lambda c, s: (0, 0, 0), pipeline_mode=pl.Buffered(1))],
            out_specs=pl.BlockSpec(memory_space=pltpu.VMEM),
            scratch_shapes=[
                pltpu.VMEM((blocks, depth * parts, LANES), jnp.float32),
                pltpu.VMEM((blocks * width, 4 * depth), jnp.bfloat16),
                pltpu.VMEM((blocks // 2, 4 * depth, 2 * LANES), jnp.bfloat16),
                pltpu.VMEM((blocks * width, LANES), jnp.float32),
                pltpu.VMEM((blocks // 2, 1, 2 * LANES), jnp.float32),
            ],
        ),
        out_shape=jax.ShapeDtypeStruct((blocks * channels * per_owner, width, 2 * width), jnp.bfloat16),
        compiler_params=pltpu.CompilerParams(vmem_limit_bytes=32 * 2**20),
        cost_estimate=pl.CostEstimate(flops=3 * 10**9, bytes_accessed=12 * 2**20, transcendentals=0),
    )(places, spectra)


def widen_kernel(tiles, out, held, sems):
    sources, channels = tiles.shape[:2]
    buffers = held.shape[0]
    copy = lambda d, n: pltpu.make_async_copy(held.at[n], out.at[d], sems.at[n])

    def source(d, carry):
        n = lax.rem(d, buffers)

        @pl.when(d >= buffers)
        def _():
            copy(d - buffers, n).wait()

        def channel(c, carry):
            held[n, c] = tiles[d, c].astype(jnp.float32)
            return carry

        lax.fori_loop(0, channels, channel, 0)
        copy(d, n).start()
        return carry

    lax.fori_loop(0, sources, source, 0)
    for d in range(sources - buffers, sources):
        copy(d, d % buffers).wait()


def widen(tiles):
    buffers = 8
    return pl.pallas_call(
        widen_kernel,
        name="widen",
        in_specs=[pl.BlockSpec(memory_space=pltpu.VMEM)],
        out_specs=pl.BlockSpec(memory_space=pltpu.HBM),
        out_shape=jax.ShapeDtypeStruct(tiles.shape, jnp.float32),
        scratch_shapes=[pltpu.VMEM((buffers, *tiles.shape[1:]), jnp.float32), pltpu.SemaphoreType.DMA((buffers,))],
        compiler_params=pltpu.CompilerParams(vmem_limit_bytes=24 * 2**20),
        cost_estimate=pl.CostEstimate(flops=0, bytes_accessed=28 * 2**20, transcendentals=0),
    )(tiles)


def on_device(voltages, tile_table):
    width, local_len = voltages.shape
    blocks = lax.axis_size("inp")
    devices = blocks * lax.axis_size("chan")
    frame_total = local_len // L * lax.axis_size("chan")
    channels = NCH // devices
    per_owner = tile_table.shape[0] // blocks
    spectra, places = channelize(voltages, tile_table, blocks, channels)
    spectra = spectra.reshape(devices, 2 * channels, spectra.shape[1])
    turned = lax.all_to_all(spectra, EVERY, 0, 0, tiled=True)
    tiles = all_tiles(turned, places, per_owner, blocks, width, frame_total)
    tiles = tiles.reshape(blocks, channels, per_owner, *tiles.shape[1:])
    out = widen(lax.all_to_all(tiles, "inp", 0, 0, tiled=True))
    return out.reshape(-1, *out.shape[2:])


def solution(mesh):
    return jax.shard_map(
        on_device,
        mesh=mesh,
        in_specs=(P("inp", "chan"), P()),
        out_specs=P("chan", "inp", None, None),
        check_vma=False,
    )
```
